1024 devices in a mesh: gx: 16 (over x_hi, z), gy: 8 (over y), event: 8 (over x_lo, core).
Axes of the slice: x: 8 (x_hi: 2, x_lo: 4; x = x_hi * 4 + x_lo), y: 8, z: 8, core: 2. Of those that a mesh axis runs over, the one named last changes fastest.
Arguments:
- adjoint: float32 [8, 3, 128, 64, 128], P('event', None, 'gx', 'gy'), may hold values from -6 to 6
- velocity: float32 [8, 3, 128, 64, 128], P('event', None, 'gx', 'gy'), may hold values from -2 to 2
- forward: float32 [8, 4, 3, 128, 64, 128], P('event', None, None, 'gx', 'gy'), may hold values from -6 to 6
- receivers: int32 [8, 512], P('event'), may hold values from 0 to 1048575
- residual: float32 [8, 2, 3, 512], P('event'), may hold values from -16 to 16
- params: float32 [3, 32, 16, 32], P(None, 'gx', 'gy'), may hold values from 0.5 to 1.5
Outputs:
- adjoint_end: float32 [8, 3, 128, 64, 128], P('event', None, 'gx', 'gy')
- gradient: float32 [3, 32, 16, 32], P(None, 'gx', 'gy', 'event')
The draws below stay inside these ranges and needn't reach their ends.
Inputs may be any that keep to these rules, and one draw needn't show every extreme that they name: Flat index (x * 64 + y) * 128 + z of a receiver's cell; several receivers may share a cell.
All inputs are finite; a program needn't handle non-finite values.
Results may differ from the reference program's by a relative error of at most 0.0001.
Values sent between devices are 32-bit elements; how exact they have to be, the bound alone decides.
A program may use at most 32 MiB of HBM per device.

```python
import math
import jax
import jax.numpy as jnp
from jax import lax

NZ = 128
R = 4
STEPS = 2
RECV = 512
EVENTS = 8
NX = 128
NY = 64
NXC = 32
NYC = 16
NZC = 32


def with_ends(result, own_key, least, largest):
    spot = [jax.random.randint(jax.random.fold_in(own_key, axis), (), 0, length) for axis, length in enumerate(result.shape)]
    longest = result.shape.index(max(result.shape))
    beside = spot[:longest] + [(spot[longest] + 1) % result.shape[longest]] + spot[longest + 1:]
    return result.at[tuple(spot)].set(least).at[tuple(beside)].set(largest)


def block_levels(own_key, shape, cuts, low, top_value):
    gain, own = 1.0, jax.random.fold_in(own_key, 6)
    for dim, blocks in cuts:
        heights = jnp.exp(jax.random.uniform(jax.random.fold_in(own, dim), (blocks,), jnp.float32, low / len(cuts), top_value / len(cuts)))
        gain = gain * jnp.repeat(heights, shape[dim] // blocks).reshape([-1 if axis == dim else 1 for axis in range(len(shape))])
    return gain


def gaussian(key, dims, width, limit, pieces=(), kind=jnp.bfloat16):
    entries = jax.random.normal(key, dims, jnp.float32) * width
    if len(pieces) > 0:
        entries = block_levels(key, dims, pieces, -0.22, 0.18) * entries
    return jnp.clip(entries, min=-limit, max=limit).astype(kind)


def setup_inputs(seed: int = 0) -> dict:
    seeds = jax.random.split(jax.random.key(seed), 7)
    adjoint = gaussian(seeds[0], (EVENTS, 3, NX, NY, NZ), 1.0, 6.0, ((0, 8), (2, 16), (3, 8)), jnp.float32)
    velocity = gaussian(seeds[1], (EVENTS, 3, NX, NY, NZ), 0.3, 2.0, ((0, 8), (2, 16), (3, 8)), jnp.float32)
    forward = gaussian(seeds[2], (EVENTS, STEPS + 2, 3, NX, NY, NZ), 1.0, 6.0, ((0, 8), (3, 16), (4, 8)), jnp.float32)
    receivers = with_ends(jax.random.randint(seeds[3], (EVENTS, RECV), 0, NX * NY * NZ), jax.random.fold_in(seeds[3], 1), 0, (NX * NY * NZ) - 1).astype(jnp.int32)
    residual = gaussian(seeds[4], (EVENTS, STEPS, 3, RECV), 4.0, 16.0, ((0, 8),), jnp.float32)
    params = jnp.clip(0.5 + 1.0 * jax.random.uniform(seeds[5], (3, NXC, NYC, NZC), jnp.float32) ** block_levels(seeds[5], (3, NXC, NYC, NZC), ((1, 16), (2, 8)), -0.2, 0.2), 0.5, 1.5)
    return dict(adjoint=adjoint, velocity=velocity, forward=forward, receivers=receivers, residual=residual, params=params)


STEP_DT2 = 0.1

def derive_xy(padded):
    inner = padded[:, 1:-1, 1:-1, :]
    zpad = jnp.pad(inner, ((0, 0), (0, 0), (0, 0), (1, 1)))
    along_x = 0.5 * (padded[:, 2:, 1:-1, :] - padded[:, :-2, 1:-1, :])
    along_y = 0.5 * (padded[:, 1:-1, 2:, :] - padded[:, 1:-1, :-2, :])
    along_z = 0.5 * (zpad[:, :, :, 2:] - zpad[:, :, :, :-2])
    return (along_x, along_y, along_z)

def strain_of(along_x, along_y, along_z):
    return jnp.stack([along_x[0], along_y[1], along_z[2], 0.5 * (along_y[0] + along_x[1]), 0.5 * (along_z[0] + along_x[2]), 0.5 * (along_z[1] + along_y[2])])

def stress_of(strain, lame, shear):
    trace = strain[0] + strain[1] + strain[2]
    normal = lame[None] * trace[None] + 2.0 * shear[None] * strain[:3]
    return jnp.concatenate([normal, 2.0 * shear[None] * strain[3:]], axis=0)

def kernels(strain_adj, strain_fwd, current, accel):
    trace_adj = strain_adj[0] + strain_adj[1] + strain_adj[2]
    trace_fwd = strain_fwd[0] + strain_fwd[1] + strain_fwd[2]
    diag = lax.optimization_barrier(jnp.sum(strain_adj[:3] * strain_fwd[:3], axis=0))
    offdiag = lax.optimization_barrier(jnp.sum(strain_adj[3:] * strain_fwd[3:], axis=0))
    return jnp.stack([trace_adj * trace_fwd, 2.0 * diag + 4.0 * offdiag, lax.optimization_barrier(jnp.sum(current * accel, axis=0))])

def pad_xy(field):
    return jnp.pad(field, ((0, 0), (1, 1), (1, 1), (0, 0)))

def reference(adjoint, velocity, forward, receivers, residual, params):
    fine = jnp.repeat(jnp.repeat(jnp.repeat(params, R, axis=1), R, axis=2), R, axis=3)
    lame, shear, inv_rho = (fine[0], fine[1], 1.0 / fine[2])
    sizex, sizey, sizez = (fine.shape[1], fine.shape[2], fine.shape[3])
    finals = []
    summed = jnp.zeros(params.shape, jnp.float32)
    for event_id in range(EVENTS):
        current = adjoint[event_id]
        previous = current - velocity[event_id]
        fwd = forward[event_id]
        total = jnp.zeros((3, sizex, sizey, sizez), jnp.float32)
        for step in range(STEPS):
            both = jnp.concatenate([current, fwd[step + 1]], axis=0)
            along_x, along_y, along_z = derive_xy(pad_xy(both))
            strain_adj = strain_of(along_x[:3], along_y[:3], along_z[:3])
            strain_fwd = strain_of(along_x[3:], along_y[3:], along_z[3:])
            stress = stress_of(strain_adj, lame, shear)
            sx, sy, sz = derive_xy(pad_xy(stress))
            force = jnp.stack([sx[0] + sy[3] + sz[4], sx[3] + sy[1] + sz[5], sx[4] + sy[5] + sz[2]])
            accel = fwd[step + 2] - 2.0 * fwd[step + 1] + fwd[step]
            total = total + kernels(strain_adj, strain_fwd, current, accel)
            inject = jnp.zeros((3, sizex * sizey * sizez), jnp.float32)
            inject = inject.at[:, receivers[event_id]].add(residual[event_id, step]).reshape(3, sizex, sizey, sizez)
            following = 2.0 * current - previous + STEP_DT2 * inv_rho[None] * (force + inject)
            previous, current = (current, following)
        finals.append(current)
        coarse = total.reshape(3, sizex // R, R, sizey // R, R, sizez // R, R).sum(axis=(2, 4, 6))
        summed = summed + coarse
    scale = 1.0 / math.sqrt(R ** 3 * STEPS * EVENTS)
    return (jnp.stack(finals), summed * scale)
```

```python
import functools
import math

import jax
import jax.numpy as jnp
from jax import lax
from jax.experimental import pallas as pl
from jax.experimental.pallas import tpu as pltpu
from jax.sharding import PartitionSpec as P

STEP_DT2 = 0.1
MESH = pl.DeviceIdType.MESH
HIGHEST = lax.Precision.HIGHEST
F32 = jnp.float32
BF16 = jnp.bfloat16
B = 8
EXT = 2 * B
DIRS = [(dx, dy) for dx in (-1, 0, 1) for dy in (-1, 0, 1) if (dx, dy) != (0, 0)]
ORDER = sorted(DIRS, key=lambda d: (d[0] == 0, d[0] != 0 and d[1] != 0))


def span(d, w, own):
    if d == 0:
        return pl.ds(0, own), pl.ds(0, own)
    if d < 0:
        return pl.ds(0, w), pl.ds(own, w)
    return pl.ds(own - w, w), pl.ds(2 * own - w, w)


def kernel(sizes, adj, vel, fwd, rec, res, par, aend, grad,
           A, A1, V, F, C, C2, ZF, PF, REC, RES, OH, Q, S, E, PK, T, G,
           lsem, ssem, rsem, gssem, grsem):
    n_gx, n_gy, n_ev, depth, ratio, steps = sizes
    gx, gy, ev = lax.axis_index("gx"), lax.axis_index("gy"), lax.axis_index("event")
    has_x = {-1: gx > 0, 1: gx < n_gx - 1}
    has_y = {-1: gy > 0, 1: gy < n_gy - 1}

    def there(dx, dy):
        if dx == 0:
            return has_y[dy]
        if dy == 0:
            return has_x[dx]
        return jnp.logical_and(has_x[dx], has_y[dy])

    barrier = pltpu.get_barrier_semaphore()
    for dx, dy in ORDER:
        @pl.when(there(dx, dy))
        def _(dx=dx, dy=dy):
            pl.semaphore_signal(barrier, inc=1, device_id={"gx": gx + dx, "gy": gy + dy}, device_id_type=MESH)
    for o in range(1, n_ev):
        pl.semaphore_signal(barrier, inc=1, device_id={"event": lax.rem(ev + o, n_ev)}, device_id_type=MESH)

    own = pl.ds(0, B)
    local = [
        pltpu.make_async_copy(adj.at[0], A.at[:, own, own, :], lsem.at[0]),
        pltpu.make_async_copy(par, C.at[:, pl.ds(0, 2), pl.ds(0, 2), :], lsem.at[1]),
        pltpu.make_async_copy(vel.at[0], V.at[:, own, own, :], lsem.at[2]),
        pltpu.make_async_copy(fwd.at[0], F.at[:, :, own, own, :], lsem.at[3]),
        pltpu.make_async_copy(rec, REC, lsem.at[4]),
        pltpu.make_async_copy(res.at[0], RES, lsem.at[5]),
    ]
    for c in local:
        c.start()

    for d in (-1, 1):
        lo = B + B // 2 if d < 0 else B
        cl = 3 if d < 0 else 2
        x_fill, y_fill = pl.ds(lo, B // 2), pl.ds(lo, B // 2)

        @pl.when(jnp.logical_not(has_x[d]))
        def _(x_fill=x_fill, cl=cl, lo=lo, d=d):
            A[:, x_fill] = jnp.zeros((3, B // 2, EXT, depth), F32)
            V[:, x_fill] = jnp.zeros((3, B // 2, EXT, depth), F32)
            fx = EXT - 1 if d < 0 else B
            for t in range(1, steps + 1):
                F[t, :, fx] = jnp.zeros((3, EXT, depth), F32)
            C[:, cl] = jnp.zeros((3, 4, C.shape[3]), F32)

        @pl.when(jnp.logical_not(has_y[d]))
        def _(y_fill=y_fill, cl=cl):
            A[:, :, y_fill] = jnp.zeros((3, EXT, B // 2, depth), F32)
            V[:, :, y_fill] = jnp.zeros((3, EXT, B // 2, depth), F32)
            for t in range(1, steps + 1):
                F[t, :, :, y_fill] = jnp.zeros((3, EXT, B // 2, depth), F32)
            C[:, :, pl.ds(cl, 1)] = jnp.zeros((3, 4, 1, C.shape[3]), F32)

    count = (1 + has_x[-1].astype(jnp.int32) + has_x[1].astype(jnp.int32)) * (
        1 + has_y[-1].astype(jnp.int32) + has_y[1].astype(jnp.int32)) - 1 + n_ev - 1
    pl.semaphore_wait(barrier, count)

    def message(kind, i, dx, dy):
        corner = dx != 0 and dy != 0
        if kind == 0:
            (sx, tx), (sy, ty) = span(dx, 1, 2), span(dy, 1, 2)
            src, dst = C.at[:, sx, sy, :], C.at[:, tx, ty, :]
        elif kind == 1:
            (sx, tx), (sy, ty) = span(dx, 3 if corner else 4, B), span(dy, 4, B)
            src, dst = A.at[:, sx, sy, :], A.at[:, tx, ty, :]
        elif kind == 2:
            w = 1 if corner else 2
            (sx, tx), (sy, ty) = span(dx, w, B), span(dy, w, B)
            src, dst = V.at[:, sx, sy, :], V.at[:, tx, ty, :]
        else:
            (sx, tx), (sy, ty) = span(dx, 1, B), span(dy, 1, B)
            lv = pl.ds(1, steps)
            src, dst = F.at[lv, :, sx, sy, :], F.at[lv, :, tx, ty, :]
        return pltpu.make_async_remote_copy(
            src_ref=src, dst_ref=dst, send_sem=ssem.at[kind, i], recv_sem=rsem.at[kind, i],
            device_id={"gx": gx + dx, "gy": gy + dy}, device_id_type=MESH)

    def dirs(kind):
        return [(i, d) for i, d in enumerate(ORDER) if kind != 3 or 0 in d]

    def send(kind):
        for i, (dx, dy) in dirs(kind):
            @pl.when(there(dx, dy))
            def _(i=i, dx=dx, dy=dy):
                message(kind, i, dx, dy).start()

    def sent(kind):
        for i, (dx, dy) in dirs(kind):
            @pl.when(there(dx, dy))
            def _(i=i, dx=dx, dy=dy):
                message(kind, i, dx, dy).wait_send()

    def arrived(kind):
        for i, (dx, dy) in dirs(kind):
            @pl.when(there(-dx, -dy))
            def _(i=i, dx=dx, dy=dy):
                message(kind, i, dx, dy).wait_recv()

    local[1].wait()
    send(0)
    local[0].wait()
    send(1)
    local[2].wait()
    send(2)
    local[3].wait()
    send(3)

    local[4].wait()
    local[5].wait()
    cells = REC[...]
    all_y = B * n_gy
    cz = lax.bitwise_and(cells, depth - 1)
    cy = lax.bitwise_and(lax.shift_right_logical(cells, int(math.log2(depth))), all_y - 1)
    cx = lax.shift_right_logical(cells, int(math.log2(depth * all_y)))
    lx, ly = cx - gx * B, cy - gy * B
    half = B // 2
    near = (lx >= -half) & (lx < B + half) & (ly >= -half) & (ly < B + half)
    place = jnp.where(near, lax.bitwise_and(lx, EXT - 1) * EXT + lax.bitwise_and(ly, EXT - 1), -1)
    n_rec = cells.shape[1]
    rows = lax.broadcasted_iota(jnp.int32, (EXT * EXT, n_rec), 0)
    OH[...] = jnp.where(rows == place, 1.0, 0.0).astype(BF16)
    at_z = lax.broadcasted_iota(jnp.int32, (depth, n_rec), 0) == cz

    for n in range(steps):
        for c in range(3):
            left = 2.0 * RES[n, c:c + 1, :]
            spread = jnp.zeros((EXT * EXT, depth), F32)
            for _ in range(3):
                piece = left.astype(BF16).astype(F32)
                left = left - piece
                b = jnp.where(at_z, piece, 0.0).astype(BF16)
                spread = spread + lax.dot_general(OH[...], b, (((1,), (1,)), ((), ())), preferred_element_type=F32)
            Q[3 * n + c] = spread.reshape(EXT, EXT, depth)

    arrived(0)
    nzc = C.shape[3]
    for p in range(3):
        for k in range(4):
            C2[pl.ds(16 * p + 4 * k, 4), :] = C[p, k]
    zi = lax.broadcasted_iota(jnp.int32, (nzc, depth), 0)
    zj = lax.broadcasted_iota(jnp.int32, (nzc, depth), 1)
    widen = jnp.where(zi == zj // ratio, 1.0, 0.0)
    ZF[...] = lax.dot_general(C2[...], widen, (((1,), (0,)), ((), ())), precision=HIGHEST, preferred_element_type=F32)
    row = lax.broadcasted_iota(jnp.int32, (EXT, depth), 0)
    for p in range(3):
        for k in range(4):
            r = [ZF[pl.ds(16 * p + 4 * k + j, 1), :] for j in range(4)]
            fine = jnp.where(row < 4, r[0], jnp.where(row < 8, r[1], jnp.where(row < 12, r[2], r[3])))
            if p == 0:
                PF[0, k] = 0.5 * fine
            elif p == 1:
                PF[1, k] = fine
            else:
                outside = fine == 0.0
                PF[2, k] = jnp.where(outside, 0.0, (0.5 * STEP_DT2) / jnp.where(outside, 1.0, fine))

    lane = lax.broadcasted_iota(jnp.int32, (EXT, depth), 1)
    not_last, not_first = lane < depth - 1, lane > 0

    def along_y(f):
        return pltpu.roll(f, EXT - 1, 0) - pltpu.roll(f, 1, 0)

    def along_z(f):
        return jnp.where(not_last, pltpu.roll(f, depth - 1, 1), 0.0) - jnp.where(not_first, pltpu.roll(f, 1, 1), 0.0)

    def wrap(x):
        return lax.bitwise_and(x, EXT - 1)

    def strain2(field, x):
        up, down = wrap(x + 1), wrap(x - 1)
        mid = [field[c, x] for c in range(3)]
        dx = [field[c, up] - field[c, down] for c in range(3)]
        dy = [along_y(f) for f in mid]
        dz = [along_z(f) for f in mid]
        return dx[0], dy[1], dz[2], dy[0] + dx[1], dz[0] + dx[2], dz[1] + dy[2]

    def stress_loop(field, reach):
        def body(t, carry):
            x = wrap(t + (EXT - reach))
            e = strain2(field, x)
            k = lax.shift_right_logical(x, 2)
            hl, mu = PF[0, k], PF[1, k]
            common = hl * (e[0] + e[1] + e[2])
            hm = 0.5 * mu
            for c in range(3):
                S[c, x] = common + mu * e[c]
                S[3 + c, x] = hm * e[3 + c]
            for c in range(6):
                E[c, x] = e[c][0:B]
            return carry
        lax.fori_loop(0, B + 2 * reach, body, 0)

    def force2(x):
        up, down = wrap(x + 1), wrap(x - 1)
        fx = (S[0, up] - S[0, down]) + along_y(S[3, x]) + along_z(S[4, x])
        fy = (S[3, up] - S[3, down]) + along_y(S[1, x]) + along_z(S[5, x])
        fz = (S[4, up] - S[4, down]) + along_y(S[5, x]) + along_z(S[2, x])
        return fx, fy, fz

    def kernel_sums(field, n):
        def body(k, carry):
            acc = [jnp.zeros((B, depth), F32) for _ in range(3)]
            for j in range(ratio):
                x = ratio * k + j
                f = [v[0:B] for v in strain2(F.at[n + 1], x)]
                e = [E[c, x] for c in range(6)]
                acc[0] = acc[0] + (e[0] + e[1] + e[2]) * (f[0] + f[1] + f[2])
                acc[1] = acc[1] + 2.0 * (e[0] * f[0] + e[1] * f[1] + e[2] * f[2]) + (
                    e[3] * f[3] + e[4] * f[4] + e[5] * f[5])
                for c in range(3):
                    accel = F[n + 2, c, x, 0:B] - 2.0 * F[n + 1, c, x, 0:B] + F[n, c, x, 0:B]
                    acc[2] = acc[2] + field[c, x, 0:B] * accel
            scale = 1.0 / math.sqrt(ratio**3 * steps * n_ev)
            for m, w in enumerate((0.25, 0.25, 1.0)):
                part = acc[m] * (w * scale)
                PK[m, k] = part if n == 0 else PK[m, k] + part
            return carry
        lax.fori_loop(0, B // ratio, body, 0)

    arrived(1)
    stress_loop(A, 3)
    arrived(2)

    def advance(t, carry):
        x = wrap(t + (EXT - 2))
        push = PF[2, lax.shift_right_logical(x, 2)]
        f = force2(x)
        for c in range(3):
            A1[c, x] = A[c, x] + V[c, x] + push * (f[c] + Q[c, x])
        return carry
    lax.fori_loop(0, B + 4, advance, 0)
    arrived(3)
    kernel_sums(A, 0)

    stress_loop(A1, 1)
    kernel_sums(A1, 1)

    kind = 3 * (B // ratio) * B
    ri = lax.broadcasted_iota(jnp.int32, (16, kind), 0)
    ci = lax.broadcasted_iota(jnp.int32, (16, kind), 1)
    pick = jnp.where(ri == ci // ratio, 1.0, 0.0)
    rowsum = lax.dot_general(pick, PK[...].reshape(kind, depth), (((1,), (0,)), ((), ())), precision=HIGHEST,
                             preferred_element_type=F32)
    wide = jnp.concatenate([rowsum[0:8], rowsum[8:16]], axis=1)
    wi = lax.broadcasted_iota(jnp.int32, (2 * depth, depth), 0)
    wj = lax.broadcasted_iota(jnp.int32, (2 * depth, depth), 1)
    narrow = jnp.where(wi // ratio == wj, 1.0, 0.0)
    T[...] = lax.dot_general(wide, narrow, (((1,), (0,)), ((), ())), precision=HIGHEST, preferred_element_type=F32)
    parts = [pltpu.make_async_remote_copy(
        src_ref=T, dst_ref=G.at[o], send_sem=gssem.at[o], recv_sem=grsem.at[o],
        device_id={"event": lax.rem(ev + o, n_ev)}, device_id_type=MESH) for o in range(1, n_ev)]
    for c in parts:
        c.start()

    def finish(x, carry):
        push = PF[2, lax.shift_right_logical(x, 2)]
        f = force2(x)
        for c in range(3):
            new = 2.0 * A1[c, x] - A[c, x] + push * (f[c] + Q[3 + c, x])
            aend[0, c, x] = new[0:B]
        return carry
    lax.fori_loop(0, B, finish, 0)

    total = T[...]
    for o, c in enumerate(parts):
        c.wait_recv()
        total = total + G[o + 1]
    width = nzc // n_ev
    mine = pltpu.roll(total, lax.rem(depth - width * ev, depth), 1)
    other = pltpu.roll(mine, depth - nzc, 1)
    for m in range(3):
        for k in range(2):
            r = 4 * m + 2 * k
            src = mine if r < 8 else other
            grad[m, k] = src[r % 8:r % 8 + 2, 0:width]

    for c in parts:
        c.wait_send()
    for kind_id in range(4):
        sent(kind_id)


def solution(mesh):
    n_gx, n_gy, n_ev = mesh.shape["gx"], mesh.shape["gy"], mesh.shape["event"]

    def on_device(adjoint, velocity, forward, receivers, residual, params):
        depth = adjoint.shape[-1]
        ratio = adjoint.shape[2] // params.shape[1]
        levels = forward.shape[1]
        steps = levels - 2
        nzc = params.shape[3]
        n_rec = receivers.shape[1]
        sizes = (n_gx, n_gy, n_ev, depth, ratio, steps)
        vm = pltpu.VMEM
        return pl.pallas_call(
            functools.partial(kernel, sizes),
            out_shape=(
                jax.ShapeDtypeStruct(adjoint.shape, F32),
                jax.ShapeDtypeStruct((3, params.shape[1], params.shape[2], nzc // n_ev), F32),
            ),
            in_specs=[pl.BlockSpec(memory_space=pl.ANY)] * 6,
            out_specs=(pl.BlockSpec(memory_space=pltpu.VMEM), pl.BlockSpec(memory_space=pltpu.VMEM)),
            scratch_shapes=[
                vm((3, EXT, EXT, depth), F32),
                vm((3, EXT, EXT, depth), F32),
                vm((3, EXT, EXT, depth), F32),
                vm((levels, 3, EXT, EXT, depth), F32),
                vm((3, 4, 4, nzc), F32),
                vm((48, nzc), F32),
                vm((48, depth), F32),
                vm((3, 4, EXT, depth), F32),
                vm((1, n_rec), jnp.int32),
                vm((steps, 3, n_rec), F32),
                vm((EXT * EXT, n_rec), BF16),
                vm((3 * steps, EXT, EXT, depth), F32),
                vm((6, EXT, EXT, depth), F32),
                vm((6, EXT, B, depth), F32),
                vm((3, B // ratio, B, depth), F32),
                vm((8, depth), F32),
                vm((n_ev, 8, depth), F32),
                pltpu.SemaphoreType.DMA((6,)),
                pltpu.SemaphoreType.DMA((4, 8)),
                pltpu.SemaphoreType.DMA((4, 8)),
                pltpu.SemaphoreType.DMA((n_ev,)),
                pltpu.SemaphoreType.DMA((n_ev,)),
            ],
            compiler_params=pltpu.CompilerParams(collective_id=0, has_side_effects=True),
        )(adjoint, velocity, forward, receivers, residual, params)

    return jax.shard_map(
        on_device,
        mesh=mesh,
        in_specs=(
            P("event", None, "gx", "gy", None),
            P("event", None, "gx", "gy", None),
            P("event", None, None, "gx", "gy", None),
            P("event", None),
            P("event", None, None, None),
            P(None, "gx", "gy", None),
        ),
        out_specs=(P("event", None, "gx", "gy", None), P(None, "gx", "gy", "event")),
        check_vma=False,
    )
```

```python
import functools
import math

import jax
import jax.numpy as jnp
from jax import lax
from jax.experimental import pallas as pl
from jax.experimental.pallas import tpu as pltpu
from jax.sharding import PartitionSpec as P

STEP_DT2 = 0.1
MESH = pl.DeviceIdType.MESH
HIGHEST = lax.Precision.HIGHEST
F32 = jnp.float32
BF16 = jnp.bfloat16
B = 8
EXT = 2 * B
DIRS = [(dx, dy) for dx in (-1, 0, 1) for dy in (-1, 0, 1) if (dx, dy) != (0, 0)]
ORDER = sorted(DIRS, key=lambda d: (d[0] == 0, d[0] != 0 and d[1] != 0))


def span(d, w, own):
    if d == 0:
        return pl.ds(0, own), pl.ds(0, own)
    if d < 0:
        return pl.ds(0, w), pl.ds(own, w)
    return pl.ds(own - w, w), pl.ds(2 * own - w, w)


def kernel(sizes, adj, vel, fwd, rec, res, par, aend, grad,
           A, A1, V, F, C, C2, ZF, PF, REC, RES, OH, Q, S0, S1, E0, E1, FS, AC, KX, T, G,
           lsem, ssem, rsem, gssem, grsem):
    n_gx, n_gy, n_ev, depth, ratio, steps = sizes
    gx, gy, ev = lax.axis_index("gx"), lax.axis_index("gy"), lax.axis_index("event")
    has_x = {-1: gx > 0, 1: gx < n_gx - 1}
    has_y = {-1: gy > 0, 1: gy < n_gy - 1}

    def there(dx, dy):
        if dx == 0:
            return has_y[dy]
        if dy == 0:
            return has_x[dx]
        return jnp.logical_and(has_x[dx], has_y[dy])

    barrier = pltpu.get_barrier_semaphore()
    for dx, dy in ORDER:
        @pl.when(there(dx, dy))
        def _(dx=dx, dy=dy):
            pl.semaphore_signal(barrier, inc=1, device_id={"gx": gx + dx, "gy": gy + dy}, device_id_type=MESH)
    for o in range(1, n_ev):
        pl.semaphore_signal(barrier, inc=1, device_id={"event": lax.rem(ev + o, n_ev)}, device_id_type=MESH)

    own = pl.ds(0, B)
    local = [
        pltpu.make_async_copy(adj.at[0], A.at[:, own, own, :], lsem.at[0]),
        pltpu.make_async_copy(par, C.at[:, pl.ds(0, 2), pl.ds(0, 2), :], lsem.at[1]),
        pltpu.make_async_copy(vel.at[0], V.at[:, own, own, :], lsem.at[2]),
        pltpu.make_async_copy(fwd.at[0], F.at[:, :, own, own, :], lsem.at[3]),
        pltpu.make_async_copy(rec, REC, lsem.at[4]),
        pltpu.make_async_copy(res.at[0], RES, lsem.at[5]),
    ]
    for c in local:
        c.start()

    for d in (-1, 1):
        lo = B + B // 2 if d < 0 else B
        cl = 3 if d < 0 else 2
        x_fill, y_fill = pl.ds(lo, B // 2), pl.ds(lo, B // 2)

        @pl.when(jnp.logical_not(has_x[d]))
        def _(x_fill=x_fill, cl=cl, lo=lo, d=d):
            A[:, x_fill] = jnp.zeros((3, B // 2, EXT, depth), F32)
            V[:, x_fill] = jnp.zeros((3, B // 2, EXT, depth), F32)
            fx = EXT - 1 if d < 0 else B
            for t in range(1, steps + 1):
                F[t, :, fx] = jnp.zeros((3, EXT, depth), F32)
            C[:, cl] = jnp.zeros((3, 4, C.shape[3]), F32)

        @pl.when(jnp.logical_not(has_y[d]))
        def _(y_fill=y_fill, cl=cl):
            A[:, :, y_fill] = jnp.zeros((3, EXT, B // 2, depth), F32)
            V[:, :, y_fill] = jnp.zeros((3, EXT, B // 2, depth), F32)
            for t in range(1, steps + 1):
                F[t, :, :, y_fill] = jnp.zeros((3, EXT, B // 2, depth), F32)
            C[:, :, pl.ds(cl, 1)] = jnp.zeros((3, 4, 1, C.shape[3]), F32)

    count = (1 + has_x[-1].astype(jnp.int32) + has_x[1].astype(jnp.int32)) * (
        1 + has_y[-1].astype(jnp.int32) + has_y[1].astype(jnp.int32)) - 1 + n_ev - 1
    pl.semaphore_wait(barrier, count)

    def message(kind, i, dx, dy):
        corner = dx != 0 and dy != 0
        if kind == 0:
            (sx, tx), (sy, ty) = span(dx, 1, 2), span(dy, 1, 2)
            src, dst = par.at[:, sx, sy, :], C.at[:, tx, ty, :]
        elif kind == 1:
            w = 3 if corner else 4
            (sx, tx), (sy, ty) = span(dx, w, B), span(dy, w, B)
            src, dst = adj.at[0, :, sx, sy, :], A.at[:, tx, ty, :]
        elif kind == 2:
            w = 1 if corner else 2
            (sx, tx), (sy, ty) = span(dx, w, B), span(dy, w, B)
            src, dst = vel.at[0, :, sx, sy, :], V.at[:, tx, ty, :]
        else:
            (sx, tx), (sy, ty) = span(dx, 1, B), span(dy, 1, B)
            lv = pl.ds(1, steps)
            src, dst = fwd.at[0, lv, :, sx, sy, :], F.at[lv, :, tx, ty, :]
        return pltpu.make_async_remote_copy(
            src_ref=src, dst_ref=dst, send_sem=ssem.at[kind, i], recv_sem=rsem.at[kind, i],
            device_id={"gx": gx + dx, "gy": gy + dy}, device_id_type=MESH)

    def dirs(kind):
        return [(i, d) for i, d in enumerate(ORDER) if kind != 3 or 0 in d]

    def send(kind):
        for i, (dx, dy) in dirs(kind):
            @pl.when(there(dx, dy))
            def _(i=i, dx=dx, dy=dy):
                message(kind, i, dx, dy).start()

    def sent(kind):
        for i, (dx, dy) in dirs(kind):
            @pl.when(there(dx, dy))
            def _(i=i, dx=dx, dy=dy):
                message(kind, i, dx, dy).wait_send()

    def arrived(kind, from_x):
        for i, (dx, dy) in dirs(kind):
            if (dx != 0) != from_x:
                continue

            @pl.when(there(-dx, -dy))
            def _(i=i, dx=dx, dy=dy):
                message(kind, i, dx, dy).wait_recv()

    for kind_id in range(4):
        send(kind_id)

    local[4].wait()
    local[5].wait()
    cells = REC[...]
    all_y = B * n_gy
    cz = lax.bitwise_and(cells, depth - 1)
    cy = lax.bitwise_and(lax.shift_right_logical(cells, int(math.log2(depth))), all_y - 1)
    cx = lax.shift_right_logical(cells, int(math.log2(depth * all_y)))
    lx, ly = cx - gx * B, cy - gy * B
    half = B // 2
    near = (lx >= -half) & (lx < B + half) & (ly >= -half) & (ly < B + half)
    place = jnp.where(near, lax.bitwise_and(lx, EXT - 1) * EXT + lax.bitwise_and(ly, EXT - 1), -1)
    n_rec = cells.shape[1]
    rows = lax.broadcasted_iota(jnp.int32, (EXT * EXT, n_rec), 0)
    OH[...] = jnp.where(rows == place, 1.0, 0.0).astype(BF16)
    at_z = lax.broadcasted_iota(jnp.int32, (depth, n_rec), 0) == cz

    for n in range(steps):
        for c in range(3):
            left = 2.0 * RES[c, n:n + 1, :]
            spread = jnp.zeros((EXT * EXT, depth), F32)
            for _ in range(3):
                piece = left.astype(BF16).astype(F32)
                left = left - piece
                b = jnp.where(at_z, piece, 0.0).astype(BF16)
                spread = spread + lax.dot_general(OH[...], b, (((1,), (1,)), ((), ())), preferred_element_type=F32)
            Q[3 * n + c] = spread.reshape(EXT, EXT, depth)

    nzc = C.shape[3]
    zi = lax.broadcasted_iota(jnp.int32, (nzc, depth), 0)
    zj = lax.broadcasted_iota(jnp.int32, (nzc, depth), 1)
    widen = jnp.where(zi == zj // ratio, 1.0, 0.0)
    row = lax.broadcasted_iota(jnp.int32, (EXT, depth), 0)

    def constants(part):
        for k in range(2 * part, 2 * part + 2):
            for p in range(3):
                C2[pl.ds(12 * k + 4 * p, 4), :] = C[p, k]
        here = pl.ds(24 * part, 24)
        ZF[here] = lax.dot_general(C2[here], widen, (((1,), (0,)), ((), ())), precision=HIGHEST,
                                   preferred_element_type=F32)
        for k in range(2 * part, 2 * part + 2):
            for p in range(3):
                r = [ZF[pl.ds(12 * k + 4 * p + j, 1), :] for j in range(4)]
                fine = jnp.where(row < 4, r[0], jnp.where(row < 8, r[1], jnp.where(row < 12, r[2], r[3])))
                if p == 0:
                    PF[0, k] = 0.5 * fine
                elif p == 1:
                    PF[1, k] = fine
                else:
                    outside = fine == 0.0
                    PF[2, k] = jnp.where(outside, 0.0, (0.5 * STEP_DT2) / jnp.where(outside, 1.0, fine))

    lane = lax.broadcasted_iota(jnp.int32, (EXT, depth), 1)
    not_last, not_first = lane < depth - 1, lane > 0

    def along_y(f):
        return pltpu.roll(f, EXT - 1, 0) - pltpu.roll(f, 1, 0)

    def along_z(f):
        return jnp.where(not_last, pltpu.roll(f, depth - 1, 1), 0.0) - jnp.where(not_first, pltpu.roll(f, 1, 1), 0.0)

    def wrap(x):
        return lax.bitwise_and(x, EXT - 1)

    def inner(lo, hi, body):
        lax.fori_loop(0, hi - lo, lambda t, c: (body(t + lo), c)[1], 0, unroll=2)

    def outer(lo, hi, reach, body):
        below = lo + reach
        above = B + reach - hi
        skip = EXT - B - 2 * reach

        def step(t, carry):
            body(wrap(t + hi + jnp.where(t >= above, skip, 0)))
            return carry
        lax.fori_loop(0, below + above, step, 0, unroll=2)

    def strain2(field, x):
        up, down = wrap(x + 1), wrap(x - 1)
        mid = [field[c, x] for c in range(3)]
        dx = [field[c, up] - field[c, down] for c in range(3)]
        dy = [along_y(f) for f in mid]
        dz = [along_z(f) for f in mid]
        return dx[0], dy[1], dz[2], dy[0] + dx[1], dz[0] + dx[2], dz[1] + dy[2]

    def stress(field, S, E):
        def body(x):
            e = strain2(field, x)
            k = lax.shift_right_logical(x, 2)
            hl, mu = PF[0, k], PF[1, k]
            common = hl * (e[0] + e[1] + e[2])
            hm = 0.5 * mu
            for c in range(3):
                S[c, x] = common + mu * e[c]
                S[3 + c, x] = hm * e[3 + c]
            for c in range(6):
                E[c, x] = e[c][0:B]
        return body

    def force2(S, x):
        up, down = wrap(x + 1), wrap(x - 1)
        fx = (S[0, up] - S[0, down]) + along_y(S[3, x]) + along_z(S[4, x])
        fy = (S[3, up] - S[3, down]) + along_y(S[1, x]) + along_z(S[5, x])
        fz = (S[4, up] - S[4, down]) + along_y(S[5, x]) + along_z(S[2, x])
        return fx, fy, fz

    def advance(x):
        push = PF[2, lax.shift_right_logical(x, 2)]
        f = force2(S0, x)
        for c in range(3):
            A1[c, x] = A[c, x] + V[c, x] + push * (f[c] + Q[c, x])

    def forward_strain(x):
        for n in range(steps):
            f = strain2(F.at[n + 1], x)
            for c in range(6):
                FS[n, c, x] = f[c][0:B]

    def acceleration(x):
        for n in range(steps):
            for c in range(3):
                AC[n, c, x] = F[n + 2, c, x, 0:B] - 2.0 * F[n + 1, c, x, 0:B] + F[n, c, x, 0:B]

    scale = 1.0 / math.sqrt(ratio**3 * steps * n_ev)

    def kernel_sums(field, E, n):
        def body(x):
            e = [E[c, x] for c in range(6)]
            f = [FS[n, c, x] for c in range(6)]
            both = (e[0] + e[1] + e[2]) * (f[0] + f[1] + f[2])
            pure = 2.0 * (e[0] * f[0] + e[1] * f[1] + e[2] * f[2]) + (e[3] * f[3] + e[4] * f[4] + e[5] * f[5])
            move = field[0, x, 0:B] * AC[n, 0, x] + field[1, x, 0:B] * AC[n, 1, x] + field[2, x, 0:B] * AC[n, 2, x]
            for m, (v, w) in enumerate(((both, 0.25), (pure, 0.25), (move, 1.0))):
                v = v * (w * scale)
                KX[m, x] = v if n == 0 else KX[m, x] + v
        return body

    for c in local[:4]:
        c.wait()
    inner(0, B, acceleration)
    for kind_id in range(2):
        arrived(kind_id, False)
    constants(0)
    inner(1, B - 1, stress(A, S0, E0))
    arrived(2, False)
    inner(2, B - 2, advance)
    inner(3, B - 3, stress(A1, S1, E1))
    arrived(3, False)
    inner(1, B - 1, forward_strain)
    inner(1, B - 1, kernel_sums(A, E0, 0))
    inner(3, B - 3, kernel_sums(A1, E1, 1))

    arrived(0, True)
    constants(1)
    arrived(1, True)
    outer(1, B - 1, 3, stress(A, S0, E0))
    arrived(2, True)
    outer(2, B - 2, 2, advance)
    outer(3, B - 3, 1, stress(A1, S1, E1))
    arrived(3, True)
    outer(1, B - 1, 0, forward_strain)
    outer(1, B - 1, 0, kernel_sums(A, E0, 0))
    outer(3, B - 3, 0, kernel_sums(A1, E1, 1))

    kind = 3 * B * B
    ri = lax.broadcasted_iota(jnp.int32, (16, kind), 0)
    ci = lax.broadcasted_iota(jnp.int32, (16, kind), 1)
    pick = jnp.where(ri == (ci // (ratio * B)) * (B // ratio) + (ci % B) // ratio, 1.0, 0.0)
    rowsum = lax.dot_general(pick, KX[...].reshape(kind, depth), (((1,), (0,)), ((), ())), precision=HIGHEST,
                             preferred_element_type=F32)
    wide = jnp.concatenate([rowsum[0:8], rowsum[8:16]], axis=1)
    wi = lax.broadcasted_iota(jnp.int32, (2 * depth, depth), 0)
    wj = lax.broadcasted_iota(jnp.int32, (2 * depth, depth), 1)
    narrow = jnp.where(wi // ratio == wj, 1.0, 0.0)
    T[...] = lax.dot_general(wide, narrow, (((1,), (0,)), ((), ())), precision=HIGHEST, preferred_element_type=F32)
    parts = [pltpu.make_async_remote_copy(
        src_ref=T, dst_ref=G.at[o], send_sem=gssem.at[o], recv_sem=grsem.at[o],
        device_id={"event": lax.rem(ev + o, n_ev)}, device_id_type=MESH) for o in range(1, n_ev)]
    for c in parts:
        c.start()

    def finish(x):
        push = PF[2, lax.shift_right_logical(x, 2)]
        f = force2(S1, x)
        for c in range(3):
            new = 2.0 * A1[c, x] - A[c, x] + push * (f[c] + Q[3 + c, x])
            aend[0, c, x] = new[0:B]
    inner(0, B, finish)

    total = T[...]
    for o, c in enumerate(parts):
        c.wait_recv()
        total = total + G[o + 1]
    width = nzc // n_ev
    mine = pltpu.roll(total, lax.rem(depth - width * ev, depth), 1)
    other = pltpu.roll(mine, depth - nzc, 1)
    for m in range(3):
        for k in range(2):
            r = 4 * m + 2 * k
            src = mine if r < 8 else other
            grad[m, k] = src[r % 8:r % 8 + 2, 0:width]

    for c in parts:
        c.wait_send()
    for kind_id in range(4):
        sent(kind_id)


def solution(mesh):
    n_gx, n_gy, n_ev = mesh.shape["gx"], mesh.shape["gy"], mesh.shape["event"]

    def on_device(adjoint, velocity, forward, receivers, residual, params):
        depth = adjoint.shape[-1]
        ratio = adjoint.shape[2] // params.shape[1]
        levels = forward.shape[1]
        steps = levels - 2
        nzc = params.shape[3]
        n_rec = receivers.shape[1]
        sizes = (n_gx, n_gy, n_ev, depth, ratio, steps)
        vm = pltpu.VMEM
        return pl.pallas_call(
            functools.partial(kernel, sizes),
            out_shape=(
                pltpu.VMEM(adjoint.shape, F32),
                pltpu.VMEM((3, params.shape[1], params.shape[2], nzc // n_ev), F32),
            ),
            in_specs=[pl.BlockSpec(memory_space=pl.ANY)] * 6,
            out_specs=(pl.BlockSpec(memory_space=pltpu.VMEM), pl.BlockSpec(memory_space=pltpu.VMEM)),
            scratch_shapes=[
                vm((3, EXT, EXT, depth), F32),
                vm((3, EXT, EXT, depth), F32),
                vm((3, EXT, EXT, depth), F32),
                vm((levels, 3, EXT, EXT, depth), F32),
                vm((3, 4, 4, nzc), F32),
                vm((48, nzc), F32),
                vm((48, depth), F32),
                vm((3, 4, EXT, depth), F32),
                vm((1, n_rec), jnp.int32),
                vm((3, steps, n_rec), F32),
                vm((EXT * EXT, n_rec), BF16),
                vm((3 * steps, EXT, EXT, depth), F32),
                vm((6, EXT, EXT, depth), F32),
                vm((6, EXT, EXT, depth), F32),
                vm((6, EXT, B, depth), F32),
                vm((6, EXT, B, depth), F32),
                vm((steps, 6, B, B, depth), F32),
                vm((steps, 3, B, B, depth), F32),
                vm((3, B, B, depth), F32),
                vm((8, depth), F32),
                vm((n_ev, 8, depth), F32),
                pltpu.SemaphoreType.DMA((6,)),
                pltpu.SemaphoreType.DMA((4, 8)),
                pltpu.SemaphoreType.DMA((4, 8)),
                pltpu.SemaphoreType.DMA((n_ev,)),
                pltpu.SemaphoreType.DMA((n_ev,)),
            ],
            compiler_params=pltpu.CompilerParams(collective_id=0, has_side_effects=True),
        )(adjoint, velocity, forward, receivers, jnp.swapaxes(residual, 1, 2), params)

    return jax.shard_map(
        on_device,
        mesh=mesh,
        in_specs=(
            P("event", None, "gx", "gy", None),
            P("event", None, "gx", "gy", None),
            P("event", None, None, "gx", "gy", None),
            P("event", None),
            P("event", None, None, None),
            P(None, "gx", "gy", None),
        ),
        out_specs=(P("event", None, "gx", "gy", None), P(None, "gx", "gy", "event")),
        check_vma=False,
    )
```

```python
import functools
import math

import jax
import jax.numpy as jnp
from jax import lax
from jax.experimental import pallas as pl
from jax.experimental.pallas import tpu as pltpu
from jax.sharding import PartitionSpec as P

STEP_DT2 = 0.1
MESH = pl.DeviceIdType.MESH
F32 = jnp.float32
BF16 = jnp.bfloat16
B = 8
EXT = 2 * B
UNROLL = 4
DIRS = [(dx, dy) for dx in (-1, 0, 1) for dy in (-1, 0, 1) if (dx, dy) != (0, 0)]
ORDER = sorted(DIRS, key=lambda d: (d[0] == 0, d[0] != 0 and d[1] != 0))


def span(d, w, own):
    if d == 0:
        return pl.ds(0, own), pl.ds(0, own)
    if d < 0:
        return pl.ds(0, w), pl.ds(own, w)
    return pl.ds(own - w, w), pl.ds(2 * own - w, w)


def times_ones(values, ones):
    pieces, left = [], values
    for _ in range(3):
        piece = left.astype(BF16)
        pieces.append(piece.astype(F32))
        left = left - pieces[-1]
    out = lax.dot_general(jnp.concatenate(pieces, axis=0).astype(BF16), ones.astype(BF16), (((1,), (0,)), ((), ())),
                          preferred_element_type=F32)
    n = values.shape[0]
    return out[0:n] + (out[n:2 * n] + out[2 * n:3 * n])


def kernel(sizes, adj, vel, fwd, rec, res, par, aend, grad,
           A, A1, V, F, C, C2, ZF, PF, REC, RES, OH, Q, S0, S1, E0, E1, FS, AC, KX, T, G,
           lsem, ssem, rsem, gssem, grsem):
    n_gx, n_gy, n_ev, depth, ratio, steps = sizes
    gx, gy, ev = lax.axis_index("gx"), lax.axis_index("gy"), lax.axis_index("event")
    has_x = {-1: gx > 0, 1: gx < n_gx - 1}
    has_y = {-1: gy > 0, 1: gy < n_gy - 1}

    def there(dx, dy):
        if dx == 0:
            return has_y[dy]
        if dy == 0:
            return has_x[dx]
        return jnp.logical_and(has_x[dx], has_y[dy])

    barrier = pltpu.get_barrier_semaphore()
    for dx, dy in ORDER:
        @pl.when(there(dx, dy))
        def _(dx=dx, dy=dy):
            pl.semaphore_signal(barrier, inc=1, device_id={"gx": gx + dx, "gy": gy + dy}, device_id_type=MESH)
    for o in range(1, n_ev):
        pl.semaphore_signal(barrier, inc=1, device_id={"event": lax.rem(ev + o, n_ev)}, device_id_type=MESH)

    own = pl.ds(0, B)
    local = [
        pltpu.make_async_copy(adj.at[0], A.at[:, own, own, :], lsem.at[0]),
        pltpu.make_async_copy(par, C.at[:, pl.ds(0, 2), pl.ds(0, 2), :], lsem.at[1]),
        pltpu.make_async_copy(vel.at[0], V.at[:, own, own, :], lsem.at[2]),
        pltpu.make_async_copy(fwd.at[0], F.at[:, :, own, own, :], lsem.at[3]),
        pltpu.make_async_copy(rec, REC, lsem.at[4]),
        pltpu.make_async_copy(res.at[0], RES, lsem.at[5]),
    ]
    for c in local:
        c.start()

    for d in (-1, 1):
        lo = B + B // 2 if d < 0 else B
        cl = 3 if d < 0 else 2
        x_fill, y_fill = pl.ds(lo, B // 2), pl.ds(lo, B // 2)

        @pl.when(jnp.logical_not(has_x[d]))
        def _(x_fill=x_fill, cl=cl, lo=lo, d=d):
            A[:, x_fill] = jnp.zeros((3, B // 2, EXT, depth), F32)
            V[:, x_fill] = jnp.zeros((3, B // 2, EXT, depth), F32)
            fx = EXT - 1 if d < 0 else B
            for t in range(1, steps + 1):
                F[t, :, fx] = jnp.zeros((3, EXT, depth), F32)
            C[:, cl] = jnp.zeros((3, 4, C.shape[3]), F32)

        @pl.when(jnp.logical_not(has_y[d]))
        def _(y_fill=y_fill, cl=cl):
            A[:, :, y_fill] = jnp.zeros((3, EXT, B // 2, depth), F32)
            V[:, :, y_fill] = jnp.zeros((3, EXT, B // 2, depth), F32)
            for t in range(1, steps + 1):
                F[t, :, :, y_fill] = jnp.zeros((3, EXT, B // 2, depth), F32)
            C[:, :, pl.ds(cl, 1)] = jnp.zeros((3, 4, 1, C.shape[3]), F32)

    count = (1 + has_x[-1].astype(jnp.int32) + has_x[1].astype(jnp.int32)) * (
        1 + has_y[-1].astype(jnp.int32) + has_y[1].astype(jnp.int32)) - 1 + n_ev - 1
    pl.semaphore_wait(barrier, count)

    def message(kind, i, dx, dy):
        corner = dx != 0 and dy != 0
        if kind == 0:
            (sx, tx), (sy, ty) = span(dx, 1, 2), span(dy, 1, 2)
            src, dst = par.at[:, sx, sy, :], C.at[:, tx, ty, :]
        elif kind == 1:
            w = 3 if corner else 4
            (sx, tx), (sy, ty) = span(dx, w, B), span(dy, w, B)
            src, dst = adj.at[0, :, sx, sy, :], A.at[:, tx, ty, :]
        elif kind == 2:
            w = 1 if corner else 2
            (sx, tx), (sy, ty) = span(dx, w, B), span(dy, w, B)
            src, dst = vel.at[0, :, sx, sy, :], V.at[:, tx, ty, :]
        else:
            (sx, tx), (sy, ty) = span(dx, 1, B), span(dy, 1, B)
            lv = pl.ds(1, steps)
            src, dst = fwd.at[0, lv, :, sx, sy, :], F.at[lv, :, tx, ty, :]
        return pltpu.make_async_remote_copy(
            src_ref=src, dst_ref=dst, send_sem=ssem.at[kind, i], recv_sem=rsem.at[kind, i],
            device_id={"gx": gx + dx, "gy": gy + dy}, device_id_type=MESH)

    def dirs(kind):
        return [(i, d) for i, d in enumerate(ORDER) if kind != 3 or 0 in d]

    def send(kind):
        for i, (dx, dy) in dirs(kind):
            @pl.when(there(dx, dy))
            def _(i=i, dx=dx, dy=dy):
                message(kind, i, dx, dy).start()

    def sent(kind):
        for i, (dx, dy) in dirs(kind):
            @pl.when(there(dx, dy))
            def _(i=i, dx=dx, dy=dy):
                message(kind, i, dx, dy).wait_send()

    def arrived(kind, from_x):
        for i, (dx, dy) in dirs(kind):
            if (dx != 0) != from_x:
                continue

            @pl.when(there(-dx, -dy))
            def _(i=i, dx=dx, dy=dy):
                message(kind, i, dx, dy).wait_recv()

    for kind_id in range(4):
        send(kind_id)

    local[4].wait()
    local[5].wait()
    cells = REC[...]
    all_y = B * n_gy
    cz = lax.bitwise_and(cells, depth - 1)
    cy = lax.bitwise_and(lax.shift_right_logical(cells, int(math.log2(depth))), all_y - 1)
    cx = lax.shift_right_logical(cells, int(math.log2(depth * all_y)))
    lx, ly = cx - gx * B, cy - gy * B
    half = B // 2
    near = (lx >= -half) & (lx < B + half) & (ly >= -half) & (ly < B + half)
    place = jnp.where(near, lax.bitwise_and(lx, EXT - 1) * EXT + lax.bitwise_and(ly, EXT - 1), -1)
    n_rec = cells.shape[1]
    rows = lax.broadcasted_iota(jnp.int32, (EXT * EXT, n_rec), 0)
    OH[...] = jnp.where(rows == place, 1.0, 0.0).astype(BF16)
    at_z = lax.broadcasted_iota(jnp.int32, (depth, n_rec), 0) == cz

    for n in range(steps):
        for c in range(3):
            left = 2.0 * RES[c, n:n + 1, :]
            spread = jnp.zeros((EXT * EXT, depth), F32)
            for _ in range(3):
                piece = left.astype(BF16).astype(F32)
                left = left - piece
                b = jnp.where(at_z, piece, 0.0).astype(BF16)
                spread = spread + lax.dot_general(OH[...], b, (((1,), (1,)), ((), ())), preferred_element_type=F32)
            Q[3 * n + c] = spread.reshape(EXT, EXT, depth)

    nzc = C.shape[3]
    zi = lax.broadcasted_iota(jnp.int32, (nzc, depth), 0)
    zj = lax.broadcasted_iota(jnp.int32, (nzc, depth), 1)
    widen = jnp.where(zi == zj // ratio, 1.0, 0.0)
    row = lax.broadcasted_iota(jnp.int32, (EXT, depth), 0)

    def constants(part):
        for k in range(2 * part, 2 * part + 2):
            for p in range(3):
                C2[pl.ds(12 * k + 4 * p, 4), :] = C[p, k]
        here = pl.ds(24 * part, 24)
        ZF[here] = times_ones(C2[here], widen)
        for k in range(2 * part, 2 * part + 2):
            for p in range(3):
                r = [ZF[pl.ds(12 * k + 4 * p + j, 1), :] for j in range(4)]
                fine = jnp.where(row < 4, r[0], jnp.where(row < 8, r[1], jnp.where(row < 12, r[2], r[3])))
                if p == 0:
                    PF[0, k] = 0.5 * fine
                elif p == 1:
                    PF[1, k] = fine
                else:
                    outside = fine == 0.0
                    PF[2, k] = jnp.where(outside, 0.0, (0.5 * STEP_DT2) / jnp.where(outside, 1.0, fine))

    lane = lax.broadcasted_iota(jnp.int32, (B, depth), 1)
    not_last, not_first = lane < depth - 1, lane > 0
    sub = lax.broadcasted_iota(jnp.int32, (B, depth), 0)
    at_top, at_end = sub == 0, sub == B - 1

    def plane(ref, *at, tiles=2):
        return [ref[(*at, pl.ds(B * t, B))] for t in range(tiles)]

    def along_y(f, tiles=2):
        out = []
        for t in range(tiles):
            a, b = f[t], f[1 - t]
            out.append(pltpu.roll(jnp.where(at_top, b, a), B - 1, 0) - pltpu.roll(jnp.where(at_end, b, a), 1, 0))
        return out

    def along_z(f, tiles=2):
        return [
            jnp.where(not_last, pltpu.roll(g, depth - 1, 1), 0.0) - jnp.where(not_first, pltpu.roll(g, 1, 1), 0.0)
            for g in f[:tiles]
        ]

    def along_x(ref, *at, tiles=2):
        *at, x = at
        up, down = plane(ref, *at, wrap(x + 1), tiles=tiles), plane(ref, *at, wrap(x - 1), tiles=tiles)
        return [a - b for a, b in zip(up, down)]

    def wrap(x):
        return lax.bitwise_and(x, EXT - 1)

    def inner(lo, hi, body):
        lax.fori_loop(0, hi - lo, lambda t, c: (body(t + lo), c)[1], 0, unroll=UNROLL)

    def outer(lo, hi, reach, body):
        below = lo + reach
        above = B + reach - hi
        skip = EXT - B - 2 * reach

        def step(t, carry):
            body(wrap(t + hi + jnp.where(t >= above, skip, 0)))
            return carry
        lax.fori_loop(0, below + above, step, 0, unroll=True)

    def strain2(field, x, tiles=2):
        mid = [plane(field, c, x) for c in range(3)]
        dx = [along_x(field, c, x, tiles=tiles) for c in range(3)]
        dy = [along_y(f, tiles) for f in mid]
        dz = [along_z(f, tiles) for f in mid]
        return [
            (dx[0][t], dy[1][t], dz[2][t], dy[0][t] + dx[1][t], dz[0][t] + dx[2][t], dz[1][t] + dy[2][t])
            for t in range(tiles)
        ]

    def stress(field, S, E):
        def body(x):
            strains = strain2(field, x)
            k = lax.shift_right_logical(x, 2)
            for t, e in enumerate(strains):
                rows_t = pl.ds(B * t, B)
                hl, mu = PF[0, k, rows_t], PF[1, k, rows_t]
                common = hl * (e[0] + e[1] + e[2])
                hm = 0.5 * mu
                for c in range(3):
                    S[c, x, rows_t] = common + mu * e[c]
                    S[3 + c, x, rows_t] = hm * e[3 + c]
            for c in range(6):
                E[c, x] = strains[0][c]
        return body

    def force2(S, x, tiles=2):
        y = [along_y(plane(S, c, x), tiles) for c in (3, 1, 5)]
        z = [along_z(plane(S, c, x), tiles) for c in (4, 5, 2)]
        d = [along_x(S, c, x, tiles=tiles) for c in (0, 3, 4)]
        return [[d[c][t] + y[c][t] + z[c][t] for c in range(3)] for t in range(tiles)]

    def advance(x):
        for t, f in enumerate(force2(S0, x)):
            rows_t = pl.ds(B * t, B)
            push = PF[2, lax.shift_right_logical(x, 2), rows_t]
            for c in range(3):
                A1[c, x, rows_t] = A[c, x, rows_t] + V[c, x, rows_t] + push * (f[c] + Q[c, x, rows_t])

    def forward_strain(x):
        for n in range(steps):
            (f,) = strain2(F.at[n + 1], x, 1)
            for c in range(6):
                FS[n, c, x] = f[c]

    def acceleration(x):
        for n in range(steps):
            for c in range(3):
                AC[n, c, x] = F[n + 2, c, x, 0:B] - 2.0 * F[n + 1, c, x, 0:B] + F[n, c, x, 0:B]

    scale = 1.0 / math.sqrt(ratio**3 * steps * n_ev)

    def kernel_sums(field, E, n):
        def body(x):
            e = [E[c, x] for c in range(6)]
            f = [FS[n, c, x] for c in range(6)]
            both = (e[0] + e[1] + e[2]) * (f[0] + f[1] + f[2])
            pure = 2.0 * (e[0] * f[0] + e[1] * f[1] + e[2] * f[2]) + (e[3] * f[3] + e[4] * f[4] + e[5] * f[5])
            move = field[0, x, 0:B] * AC[n, 0, x] + field[1, x, 0:B] * AC[n, 1, x] + field[2, x, 0:B] * AC[n, 2, x]
            for m, (v, w) in enumerate(((both, 0.25), (pure, 0.25), (move, 1.0))):
                v = v * (w * scale)
                KX[m, x] = v if n == 0 else KX[m, x] + v
        return body

    for c in local[:4]:
        c.wait()
    inner(0, B, acceleration)
    for kind_id in range(2):
        arrived(kind_id, False)
    constants(0)
    inner(1, B - 1, stress(A, S0, E0))
    arrived(2, False)
    inner(2, B - 2, advance)
    inner(3, B - 3, stress(A1, S1, E1))
    arrived(3, False)
    inner(1, B - 1, forward_strain)
    inner(1, B - 1, kernel_sums(A, E0, 0))
    inner(3, B - 3, kernel_sums(A1, E1, 1))

    arrived(0, True)
    constants(1)
    arrived(1, True)
    outer(1, B - 1, 3, stress(A, S0, E0))
    arrived(2, True)
    outer(2, B - 2, 2, advance)
    outer(3, B - 3, 1, stress(A1, S1, E1))
    arrived(3, True)
    outer(1, B - 1, 0, forward_strain)
    outer(1, B - 1, 0, kernel_sums(A, E0, 0))
    outer(3, B - 3, 0, kernel_sums(A1, E1, 1))

    sums = []
    for m in range(3):
        for k in range(B // ratio):
            v = sum(KX[m, ratio * k + j] for j in range(1, ratio)) + KX[m, ratio * k]
            v = v + pltpu.roll(v, B - 1, 0)
            sums.append(v + pltpu.roll(v, B - 2, 0))
    spot = lax.bitwise_and(sub, 3)
    halves = []
    for at in (0, 4):
        v = sums[at]
        for j in range(1, min(4, len(sums) - at)):
            v = jnp.where(spot == j, pltpu.roll(sums[at + j], j, 0), v)
        halves.append(v)
    wide = jnp.concatenate(halves, axis=1)
    wi = lax.broadcasted_iota(jnp.int32, (2 * depth, depth), 0)
    wj = lax.broadcasted_iota(jnp.int32, (2 * depth, depth), 1)
    T[...] = times_ones(wide, jnp.where(wi // ratio == wj, 1.0, 0.0))
    parts = [pltpu.make_async_remote_copy(
        src_ref=T, dst_ref=G.at[o], send_sem=gssem.at[o], recv_sem=grsem.at[o],
        device_id={"event": lax.rem(ev + o, n_ev)}, device_id_type=MESH) for o in range(1, n_ev)]
    for c in parts:
        c.start()

    def finish(x):
        (f,) = force2(S1, x, 1)
        push = PF[2, lax.shift_right_logical(x, 2), 0:B]
        for c in range(3):
            aend[0, c, x] = 2.0 * A1[c, x, 0:B] - A[c, x, 0:B] + push * (f[c] + Q[3 + c, x, 0:B])
    inner(0, B, finish)
    for kind_id in range(4):
        sent(kind_id)
    for c in parts:
        c.wait_send()

    total = T[...]
    for o, c in enumerate(parts):
        c.wait_recv()
        total = total + G[o + 1]
    width = nzc // n_ev
    mine = pltpu.roll(total, lax.rem(depth - width * ev, depth), 1)
    other = pltpu.roll(mine, depth - nzc, 1)
    for m in range(3):
        for k in range(2):
            i = 2 * m + k
            src = mine if i < 4 else other
            for y in range(2):
                grad[m, k, y:y + 1] = src[4 * y + i % 4:4 * y + i % 4 + 1, 0:width]


def put_out(aend, grad, aend_out, grad_out, sems):
    copies = [pltpu.make_async_copy(aend, aend_out, sems.at[0]), pltpu.make_async_copy(grad, grad_out, sems.at[1])]
    for c in copies:
        c.start()
    for c in copies:
        c.wait()


def solution(mesh):
    n_gx, n_gy, n_ev = mesh.shape["gx"], mesh.shape["gy"], mesh.shape["event"]

    def on_device(adjoint, velocity, forward, receivers, residual, params):
        depth = adjoint.shape[-1]
        ratio = adjoint.shape[2] // params.shape[1]
        levels = forward.shape[1]
        steps = levels - 2
        nzc = params.shape[3]
        n_rec = receivers.shape[1]
        sizes = (n_gx, n_gy, n_ev, depth, ratio, steps)
        vm = pltpu.VMEM
        held = pl.pallas_call(
            functools.partial(kernel, sizes),
            out_shape=(
                pltpu.VMEM(adjoint.shape, F32),
                pltpu.VMEM((3, params.shape[1], params.shape[2], nzc // n_ev), F32),
            ),
            in_specs=[pl.BlockSpec(memory_space=pl.ANY)] * 6,
            out_specs=(pl.BlockSpec(memory_space=pltpu.VMEM), pl.BlockSpec(memory_space=pltpu.VMEM)),
            scratch_shapes=[
                vm((3, EXT, EXT, depth), F32),
                vm((3, EXT, EXT, depth), F32),
                vm((3, EXT, EXT, depth), F32),
                vm((levels, 3, EXT, EXT, depth), F32),
                vm((3, 4, 4, nzc), F32),
                vm((48, nzc), F32),
                vm((48, depth), F32),
                vm((3, 4, EXT, depth), F32),
                vm((1, n_rec), jnp.int32),
                vm((3, steps, n_rec), F32),
                vm((EXT * EXT, n_rec), BF16),
                vm((3 * steps, EXT, EXT, depth), F32),
                vm((6, EXT, EXT, depth), F32),
                vm((6, EXT, EXT, depth), F32),
                vm((6, EXT, B, depth), F32),
                vm((6, EXT, B, depth), F32),
                vm((steps, 6, B, B, depth), F32),
                vm((steps, 3, B, B, depth), F32),
                vm((3, B, B, depth), F32),
                vm((8, depth), F32),
                vm((n_ev, 8, depth), F32),
                pltpu.SemaphoreType.DMA((6,)),
                pltpu.SemaphoreType.DMA((4, 8)),
                pltpu.SemaphoreType.DMA((4, 8)),
                pltpu.SemaphoreType.DMA((n_ev,)),
                pltpu.SemaphoreType.DMA((n_ev,)),
            ],
            compiler_params=pltpu.CompilerParams(collective_id=0, has_side_effects=True),
        )(adjoint, velocity, forward, receivers, jnp.swapaxes(residual, 1, 2), params)
        return pl.pallas_call(
            put_out,
            out_shape=tuple(jax.ShapeDtypeStruct(h.shape, F32) for h in held),
            in_specs=[pl.BlockSpec(memory_space=pltpu.VMEM)] * 2,
            out_specs=(pl.BlockSpec(memory_space=pl.ANY),) * 2,
            scratch_shapes=[pltpu.SemaphoreType.DMA((2,))],
        )(*[pltpu.with_memory_space_constraint(h, pltpu.VMEM) for h in held])

    return jax.shard_map(
        on_device,
        mesh=mesh,
        in_specs=(
            P("event", None, "gx", "gy", None),
            P("event", None, "gx", "gy", None),
            P("event", None, None, "gx", "gy", None),
            P("event", None),
            P("event", None, None, None),
            P(None, "gx", "gy", None),
        ),
        out_specs=(P("event", None, "gx", "gy", None), P(None, "gx", "gy", "event")),
        check_vma=False,
    )
```

```python
import functools
import math

import jax
import jax.numpy as jnp
from jax import lax
from jax.experimental import pallas as pl
from jax.experimental.pallas import tpu as pltpu
from jax.sharding import PartitionSpec as P

STEP_DT2 = 0.1
MESH = pl.DeviceIdType.MESH
F32 = jnp.float32
BF16 = jnp.bfloat16
B = 8
EXT = 2 * B
UNROLL = 4
DIRS = [(dx, dy) for dx in (-1, 0, 1) for dy in (-1, 0, 1) if (dx, dy) != (0, 0)]
ORDER = sorted(DIRS, key=lambda d: (d[0] == 0, d[0] != 0 and d[1] != 0))


def span(d, w, own):
    if d == 0:
        return pl.ds(0, own), pl.ds(0, own)
    if d < 0:
        return pl.ds(0, w), pl.ds(own, w)
    return pl.ds(own - w, w), pl.ds(2 * own - w, w)


def times_ones(values, ones):
    pieces, left = [], values
    for _ in range(3):
        piece = left.astype(BF16)
        pieces.append(piece.astype(F32))
        left = left - pieces[-1]
    out = lax.dot_general(jnp.concatenate(pieces, axis=0).astype(BF16), ones.astype(BF16), (((1,), (0,)), ((), ())),
                          preferred_element_type=F32)
    n = values.shape[0]
    return out[0:n] + (out[n:2 * n] + out[2 * n:3 * n])


def kernel(sizes, adj, vel, fwd, rec, res, par, aend, grad,
           A, A1, V, F, C, C2, ZF, PF, REC, RES, OH, Q, S0, S1, E0, E1, FS, AC, KX, T, G,
           lsem, ssem, rsem, gssem, grsem, gate):
    n_gx, n_gy, n_ev, depth, ratio, steps = sizes
    gx, gy, ev = lax.axis_index("gx"), lax.axis_index("gy"), lax.axis_index("event")
    has_x = {-1: gx > 0, 1: gx < n_gx - 1}
    has_y = {-1: gy > 0, 1: gy < n_gy - 1}

    def there(dx, dy):
        if dx == 0:
            return has_y[dy]
        if dy == 0:
            return has_x[dx]
        return jnp.logical_and(has_x[dx], has_y[dy])

    n_z, n_x = n_gx // 2, n_ev

    def turn(px, py, pe):
        z, y = lax.rem(px, n_z), py
        x, core = (px // n_z) * (n_ev // 2) + pe // 2, lax.rem(pe, 2)

        def hops(v, n):
            return v + (2 * v > n).astype(jnp.int32) * (n - 2 * v)
        place = ((z * n_gy + y) * n_x + x) * 2 + core
        root = (place == 0).astype(jnp.int32)
        late = 13 * place - 400 * core + 800 * (hops(z, n_z) + hops(y, n_gy) + hops(x, n_x)) + root * 20000
        return late * 2048 + place

    my_turn = turn(gx, gy, ev)
    mates = []
    for dx, dy in ORDER:
        exists = there(dx, dy)
        mates.append((exists, turn(gx + dx, gy + dy, ev) > my_turn, {"gx": gx + dx, "gy": gy + dy}))
    for o in range(1, n_ev):
        mate = lax.rem(ev + o, n_ev)
        mates.append((None, turn(gx, gy, mate) > my_turn, {"event": mate}))
    later, earlier = [], []
    for exists, after, _ in mates:
        later.append(after if exists is None else jnp.logical_and(exists, after))
        before = jnp.logical_not(after)
        earlier.append(before if exists is None else jnp.logical_and(exists, before))

    barrier = pltpu.get_barrier_semaphore()
    for (_, _, device), cond in zip(mates, later):
        @pl.when(cond)
        def _(device=device):
            pl.semaphore_signal(barrier, inc=1, device_id=device, device_id_type=MESH)
    greetings = sum(c.astype(jnp.int32) for c in earlier)

    @pl.when(greetings > 0)
    def _():
        pl.semaphore_wait(barrier, greetings)

    own = pl.ds(0, B)
    local = [
        pltpu.make_async_copy(adj.at[0], A.at[:, own, own, :], lsem.at[0]),
        pltpu.make_async_copy(par, C.at[:, pl.ds(0, 2), pl.ds(0, 2), :], lsem.at[1]),
        pltpu.make_async_copy(vel.at[0], V.at[:, own, own, :], lsem.at[2]),
        pltpu.make_async_copy(fwd.at[0], F.at[:, :, own, own, :], lsem.at[3]),
        pltpu.make_async_copy(rec, REC, lsem.at[4]),
        pltpu.make_async_copy(res.at[0], RES, lsem.at[5]),
    ]
    def message(kind, i, dx, dy):
        corner = dx != 0 and dy != 0
        if kind == 0:
            (sx, tx), (sy, ty) = span(dx, 1, 2), span(dy, 1, 2)
            src, dst = par.at[:, sx, sy, :], C.at[:, tx, ty, :]
        elif kind == 1:
            w = 3 if corner else 4
            (sx, tx), (sy, ty) = span(dx, w, B), span(dy, w, B)
            src, dst = adj.at[0, :, sx, sy, :], A.at[:, tx, ty, :]
        elif kind == 2:
            w = 1 if corner else 2
            (sx, tx), (sy, ty) = span(dx, w, B), span(dy, w, B)
            src, dst = vel.at[0, :, sx, sy, :], V.at[:, tx, ty, :]
        else:
            (sx, tx), (sy, ty) = span(dx, 1, B), span(dy, 1, B)
            lv = pl.ds(1, steps)
            src, dst = fwd.at[0, lv, :, sx, sy, :], F.at[lv, :, tx, ty, :]
        return pltpu.make_async_remote_copy(
            src_ref=src, dst_ref=dst, send_sem=ssem.at[kind, i], recv_sem=rsem.at[kind, i],
            device_id={"gx": gx + dx, "gy": gy + dy}, device_id_type=MESH)

    def dirs(kind):
        return [(i, d) for i, d in enumerate(ORDER) if kind != 3 or 0 in d]

    def send(kind, i, cond):
        dx, dy = ORDER[i]
        if kind != 3 or 0 in (dx, dy):
            @pl.when(cond)
            def _():
                message(kind, i, dx, dy).start()

    def answered(i, cond):
        @pl.when(cond)
        def _():
            pl.semaphore_wait(gate.at[i], 1)

    def send_after_answer(in_x):
        for i, (dx, dy) in enumerate(ORDER):
            if (dx != 0) == in_x:
                answered(i, later[i])
                for kind in range(4):
                    send(kind, i, later[i])

    def sent(kind):
        for i, (dx, dy) in dirs(kind):
            @pl.when(there(dx, dy))
            def _(i=i, dx=dx, dy=dy):
                message(kind, i, dx, dy).wait_send()

    def arrived(kind, from_x):
        for i, (dx, dy) in dirs(kind):
            if (dx != 0) != from_x:
                continue

            @pl.when(there(-dx, -dy))
            def _(i=i, dx=dx, dy=dy):
                message(kind, i, dx, dy).wait_recv()

    for kind in (0, 1):
        for i in range(len(ORDER)):
            send(kind, i, earlier[i])
    for i, ((_, _, device), cond) in enumerate(zip(mates, earlier)):
        other = ORDER.index(tuple(-d for d in ORDER[i])) if i < len(ORDER) else 2 * len(ORDER) + n_ev - 2 - i

        @pl.when(cond)
        def _(device=device, other=other):
            pl.semaphore_signal(gate.at[other], inc=1, device_id=device, device_id_type=MESH)
    for kind in (2, 3):
        for i in range(len(ORDER)):
            send(kind, i, earlier[i])
    for c in local:
        c.start()

    for d in (-1, 1):
        lo = B + B // 2 if d < 0 else B
        cl = 3 if d < 0 else 2
        x_fill, y_fill = pl.ds(lo, B // 2), pl.ds(lo, B // 2)

        @pl.when(jnp.logical_not(has_x[d]))
        def _(x_fill=x_fill, cl=cl, lo=lo, d=d):
            A[:, x_fill] = jnp.zeros((3, B // 2, EXT, depth), F32)
            V[:, x_fill] = jnp.zeros((3, B // 2, EXT, depth), F32)
            fx = EXT - 1 if d < 0 else B
            for t in range(1, steps + 1):
                F[t, :, fx] = jnp.zeros((3, EXT, depth), F32)
            C[:, cl] = jnp.zeros((3, 4, C.shape[3]), F32)

        @pl.when(jnp.logical_not(has_y[d]))
        def _(y_fill=y_fill, cl=cl):
            A[:, :, y_fill] = jnp.zeros((3, EXT, B // 2, depth), F32)
            V[:, :, y_fill] = jnp.zeros((3, EXT, B // 2, depth), F32)
            for t in range(1, steps + 1):
                F[t, :, :, y_fill] = jnp.zeros((3, EXT, B // 2, depth), F32)
            C[:, :, pl.ds(cl, 1)] = jnp.zeros((3, 4, 1, C.shape[3]), F32)

    send_after_answer(False)

    local[4].wait()
    local[5].wait()
    cells = REC[...]
    all_y = B * n_gy
    cz = lax.bitwise_and(cells, depth - 1)
    cy = lax.bitwise_and(lax.shift_right_logical(cells, int(math.log2(depth))), all_y - 1)
    cx = lax.shift_right_logical(cells, int(math.log2(depth * all_y)))
    lx, ly = cx - gx * B, cy - gy * B
    half = B // 2
    near = (lx >= -half) & (lx < B + half) & (ly >= -half) & (ly < B + half)
    place = jnp.where(near, lax.bitwise_and(lx, EXT - 1) * EXT + lax.bitwise_and(ly, EXT - 1), -1)
    n_rec = cells.shape[1]
    rows = lax.broadcasted_iota(jnp.int32, (EXT * EXT, n_rec), 0)
    OH[...] = jnp.where(rows == place, 1.0, 0.0).astype(BF16)
    at_z = lax.broadcasted_iota(jnp.int32, (depth, n_rec), 0) == cz

    for n in range(steps):
        for c in range(3):
            left = 2.0 * RES[c, n:n + 1, :]
            spread = jnp.zeros((EXT * EXT, depth), F32)
            for _ in range(3):
                piece = left.astype(BF16).astype(F32)
                left = left - piece
                b = jnp.where(at_z, piece, 0.0).astype(BF16)
                spread = spread + lax.dot_general(OH[...], b, (((1,), (1,)), ((), ())), preferred_element_type=F32)
            Q[3 * n + c] = spread.reshape(EXT, EXT, depth)

    send_after_answer(True)

    nzc = C.shape[3]
    zi = lax.broadcasted_iota(jnp.int32, (nzc, depth), 0)
    zj = lax.broadcasted_iota(jnp.int32, (nzc, depth), 1)
    widen = jnp.where(zi == zj // ratio, 1.0, 0.0)
    row = lax.broadcasted_iota(jnp.int32, (EXT, depth), 0)

    def constants(part):
        for k in range(2 * part, 2 * part + 2):
            for p in range(3):
                C2[pl.ds(12 * k + 4 * p, 4), :] = C[p, k]
        here = pl.ds(24 * part, 24)
        ZF[here] = times_ones(C2[here], widen)
        for k in range(2 * part, 2 * part + 2):
            for p in range(3):
                r = [ZF[pl.ds(12 * k + 4 * p + j, 1), :] for j in range(4)]
                fine = jnp.where(row < 4, r[0], jnp.where(row < 8, r[1], jnp.where(row < 12, r[2], r[3])))
                if p == 0:
                    PF[0, k] = 0.5 * fine
                elif p == 1:
                    PF[1, k] = fine
                else:
                    outside = fine == 0.0
                    PF[2, k] = jnp.where(outside, 0.0, (0.5 * STEP_DT2) / jnp.where(outside, 1.0, fine))

    lane = lax.broadcasted_iota(jnp.int32, (B, depth), 1)
    not_last, not_first = lane < depth - 1, lane > 0
    sub = lax.broadcasted_iota(jnp.int32, (B, depth), 0)
    at_top, at_end = sub == 0, sub == B - 1

    def plane(ref, *at, tiles=2):
        return [ref[(*at, pl.ds(B * t, B))] for t in range(tiles)]

    def along_y(f, tiles=2):
        out = []
        for t in range(tiles):
            a, b = f[t], f[1 - t]
            out.append(pltpu.roll(jnp.where(at_top, b, a), B - 1, 0) - pltpu.roll(jnp.where(at_end, b, a), 1, 0))
        return out

    def along_z(f, tiles=2):
        return [
            jnp.where(not_last, pltpu.roll(g, depth - 1, 1), 0.0) - jnp.where(not_first, pltpu.roll(g, 1, 1), 0.0)
            for g in f[:tiles]
        ]

    def along_x(ref, *at, tiles=2):
        *at, x = at
        up, down = plane(ref, *at, wrap(x + 1), tiles=tiles), plane(ref, *at, wrap(x - 1), tiles=tiles)
        return [a - b for a, b in zip(up, down)]

    def wrap(x):
        return lax.bitwise_and(x, EXT - 1)

    def inner(lo, hi, body):
        lax.fori_loop(0, hi - lo, lambda t, c: (body(t + lo), c)[1], 0, unroll=UNROLL)

    def outer(lo, hi, reach, body):
        below = lo + reach
        above = B + reach - hi
        skip = EXT - B - 2 * reach

        def step(t, carry):
            body(wrap(t + hi + jnp.where(t >= above, skip, 0)))
            return carry
        lax.fori_loop(0, below + above, step, 0, unroll=True)

    def strain2(field, x, tiles=2):
        mid = [plane(field, c, x) for c in range(3)]
        dx = [along_x(field, c, x, tiles=tiles) for c in range(3)]
        dy = [along_y(f, tiles) for f in mid]
        dz = [along_z(f, tiles) for f in mid]
        return [
            (dx[0][t], dy[1][t], dz[2][t], dy[0][t] + dx[1][t], dz[0][t] + dx[2][t], dz[1][t] + dy[2][t])
            for t in range(tiles)
        ]

    def stress(field, S, E):
        def body(x):
            strains = strain2(field, x)
            k = lax.shift_right_logical(x, 2)
            for t, e in enumerate(strains):
                rows_t = pl.ds(B * t, B)
                hl, mu = PF[0, k, rows_t], PF[1, k, rows_t]
                common = hl * (e[0] + e[1] + e[2])
                hm = 0.5 * mu
                for c in range(3):
                    S[c, x, rows_t] = common + mu * e[c]
                    S[3 + c, x, rows_t] = hm * e[3 + c]
            for c in range(6):
                E[c, x] = strains[0][c]
        return body

    def force2(S, x, tiles=2):
        y = [along_y(plane(S, c, x), tiles) for c in (3, 1, 5)]
        z = [along_z(plane(S, c, x), tiles) for c in (4, 5, 2)]
        d = [along_x(S, c, x, tiles=tiles) for c in (0, 3, 4)]
        return [[d[c][t] + y[c][t] + z[c][t] for c in range(3)] for t in range(tiles)]

    def advance(x):
        for t, f in enumerate(force2(S0, x)):
            rows_t = pl.ds(B * t, B)
            push = PF[2, lax.shift_right_logical(x, 2), rows_t]
            for c in range(3):
                A1[c, x, rows_t] = A[c, x, rows_t] + V[c, x, rows_t] + push * (f[c] + Q[c, x, rows_t])

    def forward_strain(x):
        for n in range(steps):
            (f,) = strain2(F.at[n + 1], x, 1)
            for c in range(6):
                FS[n, c, x] = f[c]

    def acceleration(x):
        for n in range(steps):
            for c in range(3):
                AC[n, c, x] = F[n + 2, c, x, 0:B] - 2.0 * F[n + 1, c, x, 0:B] + F[n, c, x, 0:B]

    scale = 1.0 / math.sqrt(ratio**3 * steps * n_ev)

    def kernel_sums(field, E, n):
        def body(x):
            e = [E[c, x] for c in range(6)]
            f = [FS[n, c, x] for c in range(6)]
            both = (e[0] + e[1] + e[2]) * (f[0] + f[1] + f[2])
            pure = 2.0 * (e[0] * f[0] + e[1] * f[1] + e[2] * f[2]) + (e[3] * f[3] + e[4] * f[4] + e[5] * f[5])
            move = field[0, x, 0:B] * AC[n, 0, x] + field[1, x, 0:B] * AC[n, 1, x] + field[2, x, 0:B] * AC[n, 2, x]
            for m, (v, w) in enumerate(((both, 0.25), (pure, 0.25), (move, 1.0))):
                v = v * (w * scale)
                KX[m, x] = v if n == 0 else KX[m, x] + v
        return body

    for c in local[:4]:
        c.wait()
    inner(0, B, acceleration)
    for kind_id in range(2):
        arrived(kind_id, False)
    constants(0)
    inner(1, B - 1, stress(A, S0, E0))
    arrived(2, False)
    inner(2, B - 2, advance)
    inner(3, B - 3, stress(A1, S1, E1))
    arrived(3, False)
    inner(1, B - 1, forward_strain)
    inner(1, B - 1, kernel_sums(A, E0, 0))
    inner(3, B - 3, kernel_sums(A1, E1, 1))

    arrived(0, True)
    constants(1)
    arrived(1, True)
    outer(1, B - 1, 3, stress(A, S0, E0))
    arrived(2, True)
    outer(2, B - 2, 2, advance)
    outer(3, B - 3, 1, stress(A1, S1, E1))
    arrived(3, True)
    outer(1, B - 1, 0, forward_strain)
    outer(1, B - 1, 0, kernel_sums(A, E0, 0))
    outer(3, B - 3, 0, kernel_sums(A1, E1, 1))

    sums = []
    for m in range(3):
        for k in range(B // ratio):
            v = sum(KX[m, ratio * k + j] for j in range(1, ratio)) + KX[m, ratio * k]
            v = v + pltpu.roll(v, B - 1, 0)
            sums.append(v + pltpu.roll(v, B - 2, 0))
    spot = lax.bitwise_and(sub, 3)
    halves = []
    for at in (0, 4):
        v = sums[at]
        for j in range(1, min(4, len(sums) - at)):
            v = jnp.where(spot == j, pltpu.roll(sums[at + j], j, 0), v)
        halves.append(v)
    wide = jnp.concatenate(halves, axis=1)
    wi = lax.broadcasted_iota(jnp.int32, (2 * depth, depth), 0)
    wj = lax.broadcasted_iota(jnp.int32, (2 * depth, depth), 1)
    T[...] = times_ones(wide, jnp.where(wi // ratio == wj, 1.0, 0.0))
    parts = [pltpu.make_async_remote_copy(
        src_ref=T, dst_ref=G.at[o], send_sem=gssem.at[o], recv_sem=grsem.at[o],
        device_id={"event": lax.rem(ev + o, n_ev)}, device_id_type=MESH) for o in range(1, n_ev)]
    for o, c in enumerate(parts):
        answered(len(ORDER) + o, later[len(ORDER) + o])
        c.start()

    def finish(x):
        (f,) = force2(S1, x, 1)
        push = PF[2, lax.shift_right_logical(x, 2), 0:B]
        for c in range(3):
            aend[0, c, x] = 2.0 * A1[c, x, 0:B] - A[c, x, 0:B] + push * (f[c] + Q[3 + c, x, 0:B])
    inner(0, B, finish)
    for kind_id in range(4):
        sent(kind_id)
    for c in parts:
        c.wait_send()

    total = T[...]
    for o, c in enumerate(parts):
        c.wait_recv()
        total = total + G[o + 1]
    width = nzc // n_ev
    mine = pltpu.roll(total, lax.rem(depth - width * ev, depth), 1)
    other = pltpu.roll(mine, depth - nzc, 1)
    for m in range(3):
        for k in range(2):
            i = 2 * m + k
            src = mine if i < 4 else other
            for y in range(2):
                grad[m, k, y:y + 1] = src[4 * y + i % 4:4 * y + i % 4 + 1, 0:width]


def put_out(aend, grad, aend_out, grad_out, sems):
    copies = [pltpu.make_async_copy(aend, aend_out, sems.at[0]), pltpu.make_async_copy(grad, grad_out, sems.at[1])]
    for c in copies:
        c.start()
    for c in copies:
        c.wait()


def solution(mesh):
    n_gx, n_gy, n_ev = mesh.shape["gx"], mesh.shape["gy"], mesh.shape["event"]

    def on_device(adjoint, velocity, forward, receivers, residual, params):
        depth = adjoint.shape[-1]
        ratio = adjoint.shape[2] // params.shape[1]
        levels = forward.shape[1]
        steps = levels - 2
        nzc = params.shape[3]
        n_rec = receivers.shape[1]
        sizes = (n_gx, n_gy, n_ev, depth, ratio, steps)
        vm = pltpu.VMEM
        held = pl.pallas_call(
            functools.partial(kernel, sizes),
            out_shape=(
                pltpu.VMEM(adjoint.shape, F32),
                pltpu.VMEM((3, params.shape[1], params.shape[2], nzc // n_ev), F32),
            ),
            in_specs=[pl.BlockSpec(memory_space=pl.ANY)] * 6,
            out_specs=(pl.BlockSpec(memory_space=pltpu.VMEM), pl.BlockSpec(memory_space=pltpu.VMEM)),
            scratch_shapes=[
                vm((3, EXT, EXT, depth), F32),
                vm((3, EXT, EXT, depth), F32),
                vm((3, EXT, EXT, depth), F32),
                vm((levels, 3, EXT, EXT, depth), F32),
                vm((3, 4, 4, nzc), F32),
                vm((48, nzc), F32),
                vm((48, depth), F32),
                vm((3, 4, EXT, depth), F32),
                vm((1, n_rec), jnp.int32),
                vm((3, steps, n_rec), F32),
                vm((EXT * EXT, n_rec), BF16),
                vm((3 * steps, EXT, EXT, depth), F32),
                vm((6, EXT, EXT, depth), F32),
                vm((6, EXT, EXT, depth), F32),
                vm((6, EXT, B, depth), F32),
                vm((6, EXT, B, depth), F32),
                vm((steps, 6, B, B, depth), F32),
                vm((steps, 3, B, B, depth), F32),
                vm((3, B, B, depth), F32),
                vm((8, depth), F32),
                vm((n_ev, 8, depth), F32),
                pltpu.SemaphoreType.DMA((6,)),
                pltpu.SemaphoreType.DMA((4, 8)),
                pltpu.SemaphoreType.DMA((4, 8)),
                pltpu.SemaphoreType.DMA((n_ev,)),
                pltpu.SemaphoreType.DMA((n_ev,)),
                pltpu.SemaphoreType.REGULAR((len(DIRS) + n_ev - 1,)),
            ],
            compiler_params=pltpu.CompilerParams(collective_id=0, has_side_effects=True),
        )(adjoint, velocity, forward, receivers, jnp.swapaxes(residual, 1, 2), params)
        return pl.pallas_call(
            put_out,
            out_shape=tuple(jax.ShapeDtypeStruct(h.shape, F32) for h in held),
            in_specs=[pl.BlockSpec(memory_space=pltpu.VMEM)] * 2,
            out_specs=(pl.BlockSpec(memory_space=pl.ANY),) * 2,
            scratch_shapes=[pltpu.SemaphoreType.DMA((2,))],
        )(*[pltpu.with_memory_space_constraint(h, pltpu.VMEM) for h in held])

    return jax.shard_map(
        on_device,
        mesh=mesh,
        in_specs=(
            P("event", None, "gx", "gy", None),
            P("event", None, "gx", "gy", None),
            P("event", None, None, "gx", "gy", None),
            P("event", None),
            P("event", None, None, None),
            P(None, "gx", "gy", None),
        ),
        out_specs=(P("event", None, "gx", "gy", None), P(None, "gx", "gy", "event")),
        check_vma=False,
    )
```

```python
import functools
import math

import jax
import jax.numpy as jnp
from jax import lax
from jax.experimental import pallas as pl
from jax.experimental.pallas import tpu as pltpu
from jax.sharding import PartitionSpec as P

STEP_DT2 = 0.1
MESH = pl.DeviceIdType.MESH
F32 = jnp.float32
BF16 = jnp.bfloat16
B = 8
EXT = 2 * B
UNROLL = 4
DIRS = [(dx, dy) for dx in (-1, 0, 1) for dy in (-1, 0, 1) if (dx, dy) != (0, 0)]
ORDER = sorted(DIRS, key=lambda d: (d[0] == 0, d[0] != 0 and d[1] != 0))
FACES = [i for i, d in enumerate(ORDER) if 0 in d]


def span(d, w, own):
    if d == 0:
        return pl.ds(0, own), pl.ds(0, own)
    if d < 0:
        return pl.ds(0, w), pl.ds(own, w)
    return pl.ds(own - w, w), pl.ds(2 * own - w, w)


def times_ones(values, ones):
    pieces, left = [], values
    for _ in range(3):
        piece = left.astype(BF16)
        pieces.append(piece.astype(F32))
        left = left - pieces[-1]
    out = lax.dot_general(jnp.concatenate(pieces, axis=0).astype(BF16), ones.astype(BF16), (((1,), (0,)), ((), ())),
                          preferred_element_type=F32)
    n = values.shape[0]
    return out[0:n] + (out[n:2 * n] + out[2 * n:3 * n])


def kernel(sizes, adj, vel, fwd, rec, res, par, aend, grad,
           A, A1, V, F, C, C2, ZF, PF, REC, RES, OH, Q, S0, S1, E0, E1, FS, AC, KX, T, G,
           lsem, ssem, rsem, rsem_faces, gsem, gate):
    n_gx, n_gy, n_ev, depth, ratio, steps = sizes
    gx, gy, ev = lax.axis_index("gx"), lax.axis_index("gy"), lax.axis_index("event")
    has_x = {-1: gx > 0, 1: gx < n_gx - 1}
    has_y = {-1: gy > 0, 1: gy < n_gy - 1}

    def there(dx, dy):
        if dx == 0:
            return has_y[dy]
        if dy == 0:
            return has_x[dx]
        return jnp.logical_and(has_x[dx], has_y[dy])

    n_z, n_x = n_gx // 2, n_ev

    def late(v, n, step):
        return 13 * step * v + 800 * (v + (2 * v > n).astype(jnp.int32) * (n - 2 * v)), step * v

    def add(*terms):
        return sum(t[0] for t in terms), sum(t[1] for t in terms)

    def of_gx(px, pe):
        return add(late(lax.rem(px, n_z), n_z, 2 * n_x * n_gy), late((px // n_z) * (n_ev // 2) + pe // 2, n_x, 2))

    def of_core(pe):
        core = lax.rem(pe, 2)
        return -387 * core, core

    def turn(*terms):
        when, place = add(*terms)
        return (when + (place == 0).astype(jnp.int32) * 20000) * 2048 + place

    in_gx = {d: of_gx(gx + d, ev) for d in (-1, 0, 1)}
    in_gy = {d: late(gy + d, n_gy, 2 * n_x) for d in (-1, 0, 1)}
    core = of_core(ev)
    my_turn = turn(in_gx[0], in_gy[0], core)
    mates = []
    for dx, dy in ORDER:
        mates.append((there(dx, dy), turn(in_gx[dx], in_gy[dy], core) > my_turn, {"gx": gx + dx, "gy": gy + dy}))
    for o in range(1, n_ev):
        mate = lax.rem(ev + o, n_ev)
        mates.append((None, turn(of_gx(gx, mate), in_gy[0], of_core(mate)) > my_turn, {"event": mate}))
    later, earlier = [], []
    for exists, after, _ in mates:
        later.append(after if exists is None else jnp.logical_and(exists, after))
        before = jnp.logical_not(after)
        earlier.append(before if exists is None else jnp.logical_and(exists, before))

    barrier = pltpu.get_barrier_semaphore()
    for (_, _, device), cond in zip(mates, later):
        @pl.when(cond)
        def _(device=device):
            pl.semaphore_signal(barrier, inc=1, device_id=device, device_id_type=MESH)
    greetings = sum(c.astype(jnp.int32) for c in earlier)

    @pl.when(greetings > 0)
    def _():
        pl.semaphore_wait(barrier, greetings)

    own = pl.ds(0, B)
    local = [
        pltpu.make_async_copy(adj.at[0], A.at[:, own, own, :], lsem.at[0]),
        pltpu.make_async_copy(par, C.at[:, pl.ds(0, 2), pl.ds(0, 2), :], lsem.at[1]),
        pltpu.make_async_copy(vel.at[0], V.at[:, own, own, :], lsem.at[0]),
        pltpu.make_async_copy(fwd.at[0], F.at[:, :, own, own, :], lsem.at[0]),
        pltpu.make_async_copy(rec, REC, lsem.at[2]),
        pltpu.make_async_copy(res.at[0], RES, lsem.at[3]),
    ]

    def bytes_of(ref, sem):
        return pltpu.make_async_copy(ref, ref, sem)

    def messages(kind, i):
        dx, dy = ORDER[i]
        corner = dx != 0 and dy != 0
        pairs = []

        def layer(src, dst, wx, wy, size, at=0):
            (sx, tx), (sy, ty) = span(dx, wx, size), span(dy, wy, size)
            if at:
                sx = pl.ds(size - at if dx > 0 else at - 1, 1)
                tx = pl.ds(2 * size - at if dx > 0 else size + at - 1, 1)
            pairs.append((src(sx, sy), dst(tx, ty)))

        if kind == 0:
            layer(lambda x, y: par.at[:, x, y, :], lambda x, y: C.at[:, x, y, :], 1, 1, 2)
        elif kind == 1 and corner:
            for at in (1, 2, 3):
                layer(lambda x, y: adj.at[0, :, x, y, :], lambda x, y: A.at[:, x, y, :], 1, 4 - at, B, at)
            layer(lambda x, y: vel.at[0, :, x, y, :], lambda x, y: V.at[:, x, y, :], 1, 1, B)
        elif kind == 1:
            layer(lambda x, y: adj.at[0, :, x, y, :], lambda x, y: A.at[:, x, y, :], 4, 4, B)
        elif not corner:
            levels = pl.ds(1, steps)
            layer(lambda x, y: vel.at[0, :, x, y, :], lambda x, y: V.at[:, x, y, :], 2, 2, B)
            layer(lambda x, y: fwd.at[0, levels, :, x, y, :], lambda x, y: F.at[levels, :, x, y, :], 1, 1, B)
        send_sem = ssem.at[0 if kind == 0 else 1, i]
        recv_sem = rsem_faces.at[FACES.index(i)] if kind == 2 else rsem.at[min(kind, 1), i]
        return [pltpu.make_async_remote_copy(
            src_ref=src, dst_ref=dst, send_sem=send_sem, recv_sem=recv_sem,
            device_id={"gx": gx + dx, "gy": gy + dy}, device_id_type=MESH) for src, dst in pairs]

    def wait_rows(n, sem):
        bytes_of(A1.at[:, pl.ds(0, n // B), pl.ds(0, B)] if n % B == 0 else A1.at[:, pl.ds(0, 1), pl.ds(0, n)], sem).wait()

    def send(kind, i, cond):
        @pl.when(cond)
        def _():
            for m in messages(kind, i):
                m.start()

    def sent():
        for i, d in enumerate(ORDER):
            @pl.when(there(*d))
            def _(i=i, d=d):
                messages(0, i)[0].wait_send()
                wait_rows(7 if 0 not in d else (6 + steps) * B, ssem.at[1, i])

    def arrived(kind, from_x):
        for i, (dx, dy) in enumerate(ORDER):
            corner = dx != 0 and dy != 0
            if (dx != 0) != from_x or (kind == 2 and corner):
                continue

            @pl.when(there(-dx, -dy))
            def _(i=i, corner=corner):
                if kind == 0:
                    messages(0, i)[0].wait_recv()
                elif kind == 1:
                    wait_rows(7 if corner else 4 * B, rsem.at[1, i])
                else:
                    wait_rows((2 + steps) * B, rsem_faces.at[FACES.index(i)])

    def group(i):
        return 2 if i >= len(ORDER) else int(ORDER[i][0] != 0)

    def answered(which):
        n = sum(c.astype(jnp.int32) for i, c in enumerate(later) if group(i) == which)

        @pl.when(n > 0)
        def _():
            pl.semaphore_wait(gate.at[which], n)

    def send_after_answer(which):
        answered(which)
        for kind in range(3):
            for i in range(len(ORDER)):
                if group(i) == which and (kind < 2 or 0 in ORDER[i]):
                    send(kind, i, later[i])

    for kind in (0, 1):
        for i in range(len(ORDER)):
            send(kind, i, earlier[i])
    for i, ((_, _, device), cond) in enumerate(zip(mates, earlier)):
        @pl.when(cond)
        def _(device=device, which=group(i)):
            pl.semaphore_signal(gate.at[which], inc=1, device_id=device, device_id_type=MESH)
    for i in range(len(ORDER)):
        if 0 in ORDER[i]:
            send(2, i, earlier[i])
    for c in local:
        c.start()

    for d in (-1, 1):
        lo = B + B // 2 if d < 0 else B
        cl = 3 if d < 0 else 2
        x_fill, y_fill = pl.ds(lo, B // 2), pl.ds(lo, B // 2)

        @pl.when(jnp.logical_not(has_x[d]))
        def _(x_fill=x_fill, cl=cl, lo=lo, d=d):
            A[:, x_fill] = jnp.zeros((3, B // 2, EXT, depth), F32)
            V[:, x_fill] = jnp.zeros((3, B // 2, EXT, depth), F32)
            fx = EXT - 1 if d < 0 else B
            for t in range(1, steps + 1):
                F[t, :, fx] = jnp.zeros((3, EXT, depth), F32)
            C[:, cl] = jnp.zeros((3, 4, C.shape[3]), F32)

        @pl.when(jnp.logical_not(has_y[d]))
        def _(y_fill=y_fill, cl=cl):
            A[:, :, y_fill] = jnp.zeros((3, EXT, B // 2, depth), F32)
            V[:, :, y_fill] = jnp.zeros((3, EXT, B // 2, depth), F32)
            for t in range(1, steps + 1):
                F[t, :, :, y_fill] = jnp.zeros((3, EXT, B // 2, depth), F32)
            C[:, :, pl.ds(cl, 1)] = jnp.zeros((3, 4, 1, C.shape[3]), F32)

    send_after_answer(0)

    local[4].wait()
    local[5].wait()
    cells = REC[...]
    all_y = B * n_gy
    cz = lax.bitwise_and(cells, depth - 1)
    cy = lax.bitwise_and(lax.shift_right_logical(cells, int(math.log2(depth))), all_y - 1)
    cx = lax.shift_right_logical(cells, int(math.log2(depth * all_y)))
    lx, ly = cx - gx * B, cy - gy * B
    half = B // 2
    near = (lx >= -half) & (lx < B + half) & (ly >= -half) & (ly < B + half)
    place = jnp.where(near, lax.bitwise_and(lx, EXT - 1) * EXT + lax.bitwise_and(ly, EXT - 1), -1)
    n_rec = cells.shape[1]
    rows = lax.broadcasted_iota(jnp.int32, (EXT * EXT, n_rec), 0)
    OH[...] = jnp.where(rows == place, 1.0, 0.0).astype(BF16)
    at_z = lax.broadcasted_iota(jnp.int32, (depth, n_rec), 0) == cz

    for n in range(steps):
        for c in range(3):
            left = 2.0 * RES[c, n:n + 1, :]
            spread = jnp.zeros((EXT * EXT, depth), F32)
            for _ in range(3):
                piece = left.astype(BF16).astype(F32)
                left = left - piece
                b = jnp.where(at_z, piece, 0.0).astype(BF16)
                spread = spread + lax.dot_general(OH[...], b, (((1,), (1,)), ((), ())), preferred_element_type=F32)
            Q[3 * n + c] = spread.reshape(EXT, EXT, depth)

    send_after_answer(1)

    nzc = C.shape[3]
    zi = lax.broadcasted_iota(jnp.int32, (nzc, depth), 0)
    zj = lax.broadcasted_iota(jnp.int32, (nzc, depth), 1)
    widen = jnp.where(zi == zj // ratio, 1.0, 0.0)
    row = lax.broadcasted_iota(jnp.int32, (EXT, depth), 0)

    def constants(part):
        for k in range(2 * part, 2 * part + 2):
            for p in range(3):
                C2[pl.ds(12 * k + 4 * p, 4), :] = C[p, k]
        here = pl.ds(24 * part, 24)
        ZF[here] = times_ones(C2[here], widen)
        for k in range(2 * part, 2 * part + 2):
            for p in range(3):
                r = [ZF[pl.ds(12 * k + 4 * p + j, 1), :] for j in range(4)]
                fine = jnp.where(row < 4, r[0], jnp.where(row < 8, r[1], jnp.where(row < 12, r[2], r[3])))
                if p == 0:
                    PF[0, k] = 0.5 * fine
                elif p == 1:
                    PF[1, k] = fine
                else:
                    outside = fine == 0.0
                    PF[2, k] = jnp.where(outside, 0.0, (0.5 * STEP_DT2) / jnp.where(outside, 1.0, fine))

    lane = lax.broadcasted_iota(jnp.int32, (B, depth), 1)
    not_last, not_first = lane < depth - 1, lane > 0
    sub = lax.broadcasted_iota(jnp.int32, (B, depth), 0)
    at_top, at_end = sub == 0, sub == B - 1

    def plane(ref, *at, tiles=2):
        return [ref[(*at, pl.ds(B * t, B))] for t in range(tiles)]

    def along_y(f, tiles=2):
        out = []
        for t in range(tiles):
            a, b = f[t], f[1 - t]
            out.append(pltpu.roll(jnp.where(at_top, b, a), B - 1, 0) - pltpu.roll(jnp.where(at_end, b, a), 1, 0))
        return out

    def along_z(f, tiles=2):
        return [
            jnp.where(not_last, pltpu.roll(g, depth - 1, 1), 0.0) - jnp.where(not_first, pltpu.roll(g, 1, 1), 0.0)
            for g in f[:tiles]
        ]

    def along_x(ref, *at, tiles=2):
        *at, x = at
        up, down = plane(ref, *at, wrap(x + 1), tiles=tiles), plane(ref, *at, wrap(x - 1), tiles=tiles)
        return [a - b for a, b in zip(up, down)]

    def wrap(x):
        return lax.bitwise_and(x, EXT - 1)

    def inner(lo, hi, body):
        lax.fori_loop(0, hi - lo, lambda t, c: (body(t + lo), c)[1], 0, unroll=UNROLL)

    def outer(lo, hi, reach, body):
        below = lo + reach
        above = B + reach - hi
        skip = EXT - B - 2 * reach

        def step(t, carry):
            body(wrap(t + hi + jnp.where(t >= above, skip, 0)))
            return carry
        lax.fori_loop(0, below + above, step, 0, unroll=True)

    def strain2(field, x, tiles=2):
        mid = [plane(field, c, x) for c in range(3)]
        dx = [along_x(field, c, x, tiles=tiles) for c in range(3)]
        dy = [along_y(f, tiles) for f in mid]
        dz = [along_z(f, tiles) for f in mid]
        return [
            (dx[0][t], dy[1][t], dz[2][t], dy[0][t] + dx[1][t], dz[0][t] + dx[2][t], dz[1][t] + dy[2][t])
            for t in range(tiles)
        ]

    def stress(field, S, E):
        def body(x):
            strains = strain2(field, x)
            k = lax.shift_right_logical(x, 2)
            for t, e in enumerate(strains):
                rows_t = pl.ds(B * t, B)
                hl, mu = PF[0, k, rows_t], PF[1, k, rows_t]
                common = hl * (e[0] + e[1] + e[2])
                hm = 0.5 * mu
                for c in range(3):
                    S[c, x, rows_t] = common + mu * e[c]
                    S[3 + c, x, rows_t] = hm * e[3 + c]
            for c in range(6):
                E[c, x] = strains[0][c]
        return body

    def force2(S, x, tiles=2):
        y = [along_y(plane(S, c, x), tiles) for c in (3, 1, 5)]
        z = [along_z(plane(S, c, x), tiles) for c in (4, 5, 2)]
        d = [along_x(S, c, x, tiles=tiles) for c in (0, 3, 4)]
        return [[d[c][t] + y[c][t] + z[c][t] for c in range(3)] for t in range(tiles)]

    def advance(x):
        for t, f in enumerate(force2(S0, x)):
            rows_t = pl.ds(B * t, B)
            push = PF[2, lax.shift_right_logical(x, 2), rows_t]
            for c in range(3):
                A1[c, x, rows_t] = A[c, x, rows_t] + V[c, x, rows_t] + push * (f[c] + Q[c, x, rows_t])

    def forward_strain(x):
        for n in range(steps):
            (f,) = strain2(F.at[n + 1], x, 1)
            for c in range(6):
                FS[n, c, x] = f[c]

    def acceleration(x):
        for n in range(steps):
            for c in range(3):
                AC[n, c, x] = F[n + 2, c, x, 0:B] - 2.0 * F[n + 1, c, x, 0:B] + F[n, c, x, 0:B]

    scale = 1.0 / math.sqrt(ratio**3 * steps * n_ev)

    def kernel_sums(field, E, n):
        def body(x):
            e = [E[c, x] for c in range(6)]
            f = [FS[n, c, x] for c in range(6)]
            both = (e[0] + e[1] + e[2]) * (f[0] + f[1] + f[2])
            pure = 2.0 * (e[0] * f[0] + e[1] * f[1] + e[2] * f[2]) + (e[3] * f[3] + e[4] * f[4] + e[5] * f[5])
            move = field[0, x, 0:B] * AC[n, 0, x] + field[1, x, 0:B] * AC[n, 1, x] + field[2, x, 0:B] * AC[n, 2, x]
            for m, (v, w) in enumerate(((both, 0.25), (pure, 0.25), (move, 1.0))):
                v = v * (w * scale)
                KX[m, x] = v if n == 0 else KX[m, x] + v
        return body

    local[1].wait()
    bytes_of(S0.at[:, pl.ds(0, 3 * EXT // 4)], lsem.at[0]).wait()
    inner(0, B, acceleration)
    arrived(0, False)
    arrived(1, False)
    constants(0)
    inner(1, B - 1, stress(A, S0, E0))
    arrived(2, False)
    inner(2, B - 2, advance)
    inner(3, B - 3, stress(A1, S1, E1))
    inner(1, B - 1, forward_strain)
    inner(1, B - 1, kernel_sums(A, E0, 0))
    inner(3, B - 3, kernel_sums(A1, E1, 1))

    arrived(0, True)
    constants(1)
    arrived(1, True)
    outer(1, B - 1, 3, stress(A, S0, E0))
    arrived(2, True)
    outer(2, B - 2, 2, advance)
    outer(3, B - 3, 1, stress(A1, S1, E1))
    outer(1, B - 1, 0, forward_strain)
    outer(1, B - 1, 0, kernel_sums(A, E0, 0))
    outer(3, B - 3, 0, kernel_sums(A1, E1, 1))

    sums = []
    for m in range(3):
        for k in range(B // ratio):
            v = sum(KX[m, ratio * k + j] for j in range(1, ratio)) + KX[m, ratio * k]
            v = v + pltpu.roll(v, B - 1, 0)
            sums.append(v + pltpu.roll(v, B - 2, 0))
    spot = lax.bitwise_and(sub, 3)
    halves = []
    for at in (0, 4):
        v = sums[at]
        for j in range(1, min(4, len(sums) - at)):
            v = jnp.where(spot == j, pltpu.roll(sums[at + j], j, 0), v)
        halves.append(v)
    wide = jnp.concatenate(halves, axis=1)
    wi = lax.broadcasted_iota(jnp.int32, (2 * depth, depth), 0)
    wj = lax.broadcasted_iota(jnp.int32, (2 * depth, depth), 1)
    T[...] = times_ones(wide, jnp.where(wi // ratio == wj, 1.0, 0.0))
    parts = [pltpu.make_async_remote_copy(
        src_ref=T, dst_ref=G.at[o - 1], send_sem=gsem.at[0], recv_sem=gsem.at[1],
        device_id={"event": lax.rem(ev + o, n_ev)}, device_id_type=MESH) for o in range(1, n_ev)]
    answered(2)
    for c in parts:
        c.start()

    def finish(x):
        (f,) = force2(S1, x, 1)
        push = PF[2, lax.shift_right_logical(x, 2), 0:B]
        for c in range(3):
            aend[0, c, x] = 2.0 * A1[c, x, 0:B] - A[c, x, 0:B] + push * (f[c] + Q[3 + c, x, 0:B])
    inner(0, B, finish)
    sent()
    bytes_of(G, gsem.at[0]).wait()
    bytes_of(G, gsem.at[1]).wait()
    total = T[...]
    for o in range(n_ev - 1):
        total = total + G[o]
    width = nzc // n_ev
    mine = pltpu.roll(total, lax.rem(depth - width * ev, depth), 1)
    other = pltpu.roll(mine, depth - nzc, 1)
    for m in range(3):
        for k in range(2):
            i = 2 * m + k
            src = mine if i < 4 else other
            for y in range(2):
                grad[m, k, y:y + 1] = src[4 * y + i % 4:4 * y + i % 4 + 1, 0:width]


def put_out(aend, grad, aend_out, grad_out, sems):
    copies = [pltpu.make_async_copy(aend, aend_out, sems.at[0]), pltpu.make_async_copy(grad, grad_out, sems.at[1])]
    for c in copies:
        c.start()
    for c in copies:
        c.wait()


def solution(mesh):
    n_gx, n_gy, n_ev = mesh.shape["gx"], mesh.shape["gy"], mesh.shape["event"]

    def on_device(adjoint, velocity, forward, receivers, residual, params):
        depth = adjoint.shape[-1]
        ratio = adjoint.shape[2] // params.shape[1]
        levels = forward.shape[1]
        steps = levels - 2
        nzc = params.shape[3]
        n_rec = receivers.shape[1]
        sizes = (n_gx, n_gy, n_ev, depth, ratio, steps)
        vm = pltpu.VMEM
        held = pl.pallas_call(
            functools.partial(kernel, sizes),
            out_shape=(
                pltpu.VMEM(adjoint.shape, F32),
                pltpu.VMEM((3, params.shape[1], params.shape[2], nzc // n_ev), F32),
            ),
            in_specs=[pl.BlockSpec(memory_space=pl.ANY)] * 6,
            out_specs=(pl.BlockSpec(memory_space=pltpu.VMEM), pl.BlockSpec(memory_space=pltpu.VMEM)),
            scratch_shapes=[
                vm((3, EXT, EXT, depth), F32),
                vm((3, EXT, EXT, depth), F32),
                vm((3, EXT, EXT, depth), F32),
                vm((levels, 3, EXT, EXT, depth), F32),
                vm((3, 4, 4, nzc), F32),
                vm((48, nzc), F32),
                vm((48, depth), F32),
                vm((3, 4, EXT, depth), F32),
                vm((1, n_rec), jnp.int32),
                vm((3, steps, n_rec), F32),
                vm((EXT * EXT, n_rec), BF16),
                vm((3 * steps, EXT, EXT, depth), F32),
                vm((6, EXT, EXT, depth), F32),
                vm((6, EXT, EXT, depth), F32),
                vm((6, EXT, B, depth), F32),
                vm((6, EXT, B, depth), F32),
                vm((steps, 6, B, B, depth), F32),
                vm((steps, 3, B, B, depth), F32),
                vm((3, B, B, depth), F32),
                vm((8, depth), F32),
                vm((n_ev - 1, 8, depth), F32),
                pltpu.SemaphoreType.DMA((4,)),
                pltpu.SemaphoreType.DMA((2, len(ORDER))),
                pltpu.SemaphoreType.DMA((2, len(ORDER))),
                pltpu.SemaphoreType.DMA((len(FACES),)),
                pltpu.SemaphoreType.DMA((2,)),
                pltpu.SemaphoreType.REGULAR((3,)),
            ],
            compiler_params=pltpu.CompilerParams(collective_id=0, has_side_effects=True),
        )(adjoint, velocity, forward, receivers, jnp.swapaxes(residual, 1, 2), params)
        return pl.pallas_call(
            put_out,
            out_shape=tuple(jax.ShapeDtypeStruct(h.shape, F32) for h in held),
            in_specs=[pl.BlockSpec(memory_space=pltpu.VMEM)] * 2,
            out_specs=(pl.BlockSpec(memory_space=pl.ANY),) * 2,
            scratch_shapes=[pltpu.SemaphoreType.DMA((2,))],
        )(*[pltpu.with_memory_space_constraint(h, pltpu.VMEM) for h in held])

    return jax.shard_map(
        on_device,
        mesh=mesh,
        in_specs=(
            P("event", None, "gx", "gy", None),
            P("event", None, "gx", "gy", None),
            P("event", None, None, "gx", "gy", None),
            P("event", None),
            P("event", None, None, None),
            P(None, "gx", "gy", None),
        ),
        out_specs=(P("event", None, "gx", "gy", None), P(None, "gx", "gy", "event")),
        check_vma=False,
    )
```

```python
import functools
import math

import jax
import jax.numpy as jnp
from jax import lax
from jax.experimental import pallas as pl
from jax.experimental.pallas import tpu as pltpu
from jax.sharding import PartitionSpec as P

STEP_DT2 = 0.1
MESH = pl.DeviceIdType.MESH
F32 = jnp.float32
BF16 = jnp.bfloat16
B = 8
EXT = 2 * B
UNROLL = 4
DIRS = [(dx, dy) for dx in (-1, 0, 1) for dy in (-1, 0, 1) if (dx, dy) != (0, 0)]
ORDER = sorted(DIRS, key=lambda d: (d[0] == 0, 0 in d))
FACES = [i for i, d in enumerate(ORDER) if 0 in d]


def span(d, w, own):
    if d == 0:
        return pl.ds(0, own), pl.ds(0, own)
    if d < 0:
        return pl.ds(0, w), pl.ds(own, w)
    return pl.ds(own - w, w), pl.ds(2 * own - w, w)


def times_ones(values, ones):
    pieces, left = [], values
    for _ in range(3):
        piece = left.astype(BF16)
        pieces.append(piece.astype(F32))
        left = left - pieces[-1]
    out = lax.dot_general(jnp.concatenate(pieces, axis=0).astype(BF16), ones.astype(BF16), (((1,), (0,)), ((), ())),
                          preferred_element_type=F32)
    n = values.shape[0]
    return out[0:n] + (out[n:2 * n] + out[2 * n:3 * n])


def kernel(sizes, adj, vel, fwd, rec, res, par, aend, grad,
           A, A1, V, F, C, C2, ZF, PF, REC, RES, OH, Q, S0, S1, E0, E1, FS, AC, KX, T, G,
           lsem, ssem, rsem, rsem_faces, gsem, gate):
    n_gx, n_gy, n_ev, depth, ratio, steps = sizes
    gx, gy, ev = lax.axis_index("gx"), lax.axis_index("gy"), lax.axis_index("event")
    has_x = {-1: gx > 0, 1: gx < n_gx - 1}
    has_y = {-1: gy > 0, 1: gy < n_gy - 1}

    def there(dx, dy):
        if dx == 0:
            return has_y[dy]
        if dy == 0:
            return has_x[dx]
        return jnp.logical_and(has_x[dx], has_y[dy])

    n_z, n_x = n_gx // 2, n_ev

    def late(v, n, step):
        return 13 * step * v + 800 * (v + (2 * v > n).astype(jnp.int32) * (n - 2 * v)), step * v

    def add(*terms):
        return sum(t[0] for t in terms), sum(t[1] for t in terms)

    def of_gx(px, pe):
        return add(late(lax.rem(px, n_z), n_z, 2 * n_x * n_gy), late((px // n_z) * (n_ev // 2) + pe // 2, n_x, 2))

    def of_core(pe):
        core = lax.rem(pe, 2)
        return -387 * core, core

    def turn(*terms):
        when, place = add(*terms)
        return (when + (place == 0).astype(jnp.int32) * 20000) * 2048 + place

    in_gx = {d: of_gx(gx + d, ev) for d in (-1, 0, 1)}
    in_gy = {d: late(gy + d, n_gy, 2 * n_x) for d in (-1, 0, 1)}
    core = of_core(ev)
    my_turn = turn(in_gx[0], in_gy[0], core)
    mates = []
    for dx, dy in ORDER:
        mates.append((there(dx, dy), turn(in_gx[dx], in_gy[dy], core) > my_turn, {"gx": gx + dx, "gy": gy + dy}))
    for o in range(1, n_ev):
        mate = lax.rem(ev + o, n_ev)
        mates.append((None, turn(of_gx(gx, mate), in_gy[0], of_core(mate)) > my_turn, {"event": mate}))
    later, earlier = [], []
    for exists, after, _ in mates:
        later.append(after if exists is None else jnp.logical_and(exists, after))
        before = jnp.logical_not(after)
        earlier.append(before if exists is None else jnp.logical_and(exists, before))

    barrier = pltpu.get_barrier_semaphore()
    for (_, _, device), cond in zip(mates, later):
        @pl.when(cond)
        def _(device=device):
            pl.semaphore_signal(barrier, inc=1, device_id=device, device_id_type=MESH)
    greetings = sum(c.astype(jnp.int32) for c in earlier)

    @pl.when(greetings > 0)
    def _():
        pl.semaphore_wait(barrier, greetings)

    own = pl.ds(0, B)
    local = [
        pltpu.make_async_copy(adj.at[0], A.at[:, own, own, :], lsem.at[0]),
        pltpu.make_async_copy(par, C.at[:, pl.ds(0, 2), pl.ds(0, 2), :], lsem.at[1]),
        pltpu.make_async_copy(vel.at[0], V.at[:, own, own, :], lsem.at[0]),
        pltpu.make_async_copy(fwd.at[0], F.at[:, :, own, own, :], lsem.at[0]),
        pltpu.make_async_copy(rec, REC, lsem.at[2]),
        pltpu.make_async_copy(res.at[0], RES, lsem.at[3]),
    ]

    def bytes_of(ref, sem):
        return pltpu.make_async_copy(ref, ref, sem)

    def messages(kind, i):
        dx, dy = ORDER[i]
        corner = dx != 0 and dy != 0
        pairs = []

        def layer(src, dst, wx, wy, size, at=0):
            (sx, tx), (sy, ty) = span(dx, wx, size), span(dy, wy, size)
            if at:
                sx = pl.ds(size - at if dx > 0 else at - 1, 1)
                tx = pl.ds(2 * size - at if dx > 0 else size + at - 1, 1)
            pairs.append((src(sx, sy), dst(tx, ty)))

        if kind == 0:
            layer(lambda x, y: par.at[:, x, y, :], lambda x, y: C.at[:, x, y, :], 1, 1, 2)
        elif kind == 1 and corner:
            for at in (1, 2, 3):
                layer(lambda x, y: adj.at[0, :, x, y, :], lambda x, y: A.at[:, x, y, :], 1, 4 - at, B, at)
            layer(lambda x, y: vel.at[0, :, x, y, :], lambda x, y: V.at[:, x, y, :], 1, 1, B)
        elif kind == 1:
            layer(lambda x, y: adj.at[0, :, x, y, :], lambda x, y: A.at[:, x, y, :], 4, 4, B)
        elif not corner:
            levels = pl.ds(1, steps)
            layer(lambda x, y: vel.at[0, :, x, y, :], lambda x, y: V.at[:, x, y, :], 2, 2, B)
            layer(lambda x, y: fwd.at[0, levels, :, x, y, :], lambda x, y: F.at[levels, :, x, y, :], 1, 1, B)
        send_sem = ssem.at[0 if kind == 0 else 1, i]
        recv_sem = rsem_faces.at[FACES.index(i)] if kind == 2 else rsem.at[min(kind, 1), i]
        return [pltpu.make_async_remote_copy(
            src_ref=src, dst_ref=dst, send_sem=send_sem, recv_sem=recv_sem,
            device_id={"gx": gx + dx, "gy": gy + dy}, device_id_type=MESH) for src, dst in pairs]

    def wait_rows(n, sem):
        bytes_of(A1.at[:, pl.ds(0, n // B), pl.ds(0, B)] if n % B == 0 else A1.at[:, pl.ds(0, 1), pl.ds(0, n)], sem).wait()

    def send(kind, i, cond):
        @pl.when(cond)
        def _():
            for m in messages(kind, i):
                m.start()

    def sent():
        for i, d in enumerate(ORDER):
            @pl.when(there(*d))
            def _(i=i, d=d):
                messages(0, i)[0].wait_send()
                wait_rows(7 if 0 not in d else (6 + steps) * B, ssem.at[1, i])

    def arrived(kind, from_x):
        for i, (dx, dy) in enumerate(ORDER):
            corner = dx != 0 and dy != 0
            if (dx != 0) != from_x or (kind == 2 and corner):
                continue

            @pl.when(there(-dx, -dy))
            def _(i=i, corner=corner):
                if kind == 0:
                    messages(0, i)[0].wait_recv()
                elif kind == 1:
                    wait_rows(7 if corner else 4 * B, rsem.at[1, i])
                else:
                    wait_rows((2 + steps) * B, rsem_faces.at[FACES.index(i)])

    def group(i):
        return 2 if i >= len(ORDER) else int(ORDER[i][0] != 0)

    def answered(which):
        n = sum(c.astype(jnp.int32) for i, c in enumerate(later) if group(i) == which)

        @pl.when(n > 0)
        def _():
            pl.semaphore_wait(gate.at[which], n)

    def send_after_answer(which):
        answered(which)
        for kind in range(3):
            for i in range(len(ORDER)):
                if group(i) == which and (kind < 2 or 0 in ORDER[i]):
                    send(kind, i, later[i])

    for kind in (0, 1):
        for i in range(len(ORDER)):
            send(kind, i, earlier[i])
    for i, ((_, _, device), cond) in enumerate(zip(mates, earlier)):
        @pl.when(cond)
        def _(device=device, which=group(i)):
            pl.semaphore_signal(gate.at[which], inc=1, device_id=device, device_id_type=MESH)
    for i in range(len(ORDER)):
        if 0 in ORDER[i]:
            send(2, i, earlier[i])
    for c in local:
        c.start()

    for d in (-1, 1):
        lo = B + B // 2 if d < 0 else B
        cl = 3 if d < 0 else 2
        x_fill, y_fill = pl.ds(lo, B // 2), pl.ds(lo, B // 2)

        @pl.when(jnp.logical_not(has_x[d]))
        def _(x_fill=x_fill, cl=cl, lo=lo, d=d):
            A[:, x_fill] = jnp.zeros((3, B // 2, EXT, depth), F32)
            V[:, x_fill] = jnp.zeros((3, B // 2, EXT, depth), F32)
            fx = EXT - 1 if d < 0 else B
            for t in range(1, steps + 1):
                F[t, :, fx] = jnp.zeros((3, EXT, depth), F32)
            C[:, cl] = jnp.zeros((3, 4, C.shape[3]), F32)

        @pl.when(jnp.logical_not(has_y[d]))
        def _(y_fill=y_fill, cl=cl):
            A[:, :, y_fill] = jnp.zeros((3, EXT, B // 2, depth), F32)
            V[:, :, y_fill] = jnp.zeros((3, EXT, B // 2, depth), F32)
            for t in range(1, steps + 1):
                F[t, :, :, y_fill] = jnp.zeros((3, EXT, B // 2, depth), F32)
            C[:, :, pl.ds(cl, 1)] = jnp.zeros((3, 4, 1, C.shape[3]), F32)

    send_after_answer(0)

    local[4].wait()
    local[5].wait()
    cells = REC[...]
    all_y = B * n_gy
    cz = lax.bitwise_and(cells, depth - 1)
    cy = lax.bitwise_and(lax.shift_right_logical(cells, int(math.log2(depth))), all_y - 1)
    cx = lax.shift_right_logical(cells, int(math.log2(depth * all_y)))
    lx, ly = cx - gx * B, cy - gy * B
    half = B // 2
    near = (lx >= -half) & (lx < B + half) & (ly >= -half) & (ly < B + half)
    place = jnp.where(near, lax.bitwise_and(lx, EXT - 1) * EXT + lax.bitwise_and(ly, EXT - 1), -1)
    n_rec = cells.shape[1]
    rows = lax.broadcasted_iota(jnp.int32, (EXT * EXT, n_rec), 0)
    OH[...] = jnp.where(rows == place, 1.0, 0.0).astype(BF16)
    at_z = lax.broadcasted_iota(jnp.int32, (depth, n_rec), 0) == cz

    for n in range(steps):
        for c in range(3):
            left = 2.0 * RES[c, n:n + 1, :]
            spread = jnp.zeros((EXT * EXT, depth), F32)
            for _ in range(3):
                piece = left.astype(BF16).astype(F32)
                left = left - piece
                b = jnp.where(at_z, piece, 0.0).astype(BF16)
                spread = spread + lax.dot_general(OH[...], b, (((1,), (1,)), ((), ())), preferred_element_type=F32)
            Q[3 * n + c] = spread.reshape(EXT, EXT, depth)

    send_after_answer(1)

    nzc = C.shape[3]
    zi = lax.broadcasted_iota(jnp.int32, (nzc, depth), 0)
    zj = lax.broadcasted_iota(jnp.int32, (nzc, depth), 1)
    widen = jnp.where(zi == zj // ratio, 1.0, 0.0)
    row = lax.broadcasted_iota(jnp.int32, (EXT, depth), 0)

    def constants(part):
        for k in range(2 * part, 2 * part + 2):
            for p in range(3):
                C2[pl.ds(12 * k + 4 * p, 4), :] = C[p, k]
        here = pl.ds(24 * part, 24)
        ZF[here] = times_ones(C2[here], widen)
        for k in range(2 * part, 2 * part + 2):
            for p in range(3):
                r = [ZF[pl.ds(12 * k + 4 * p + j, 1), :] for j in range(4)]
                fine = jnp.where(row < 4, r[0], jnp.where(row < 8, r[1], jnp.where(row < 12, r[2], r[3])))
                if p == 0:
                    PF[0, k] = 0.5 * fine
                elif p == 1:
                    PF[1, k] = fine
                else:
                    outside = fine == 0.0
                    PF[2, k] = jnp.where(outside, 0.0, (0.5 * STEP_DT2) / jnp.where(outside, 1.0, fine))

    lane = lax.broadcasted_iota(jnp.int32, (B, depth), 1)
    not_last, not_first = lane < depth - 1, lane > 0
    sub = lax.broadcasted_iota(jnp.int32, (B, depth), 0)
    at_top, at_end = sub == 0, sub == B - 1

    def plane(ref, *at, tiles=2):
        return [ref[(*at, pl.ds(B * t, B))] for t in range(tiles)]

    def along_y(f, tiles=2):
        out = []
        for t in range(tiles):
            a, b = f[t], f[1 - t]
            out.append(pltpu.roll(jnp.where(at_top, b, a), B - 1, 0) - pltpu.roll(jnp.where(at_end, b, a), 1, 0))
        return out

    def along_z(f, tiles=2):
        return [
            jnp.where(not_last, pltpu.roll(g, depth - 1, 1), 0.0) - jnp.where(not_first, pltpu.roll(g, 1, 1), 0.0)
            for g in f[:tiles]
        ]

    def along_x(ref, *at, tiles=2):
        *at, x = at
        up, down = plane(ref, *at, wrap(x + 1), tiles=tiles), plane(ref, *at, wrap(x - 1), tiles=tiles)
        return [a - b for a, b in zip(up, down)]

    def wrap(x):
        return lax.bitwise_and(x, EXT - 1)

    def inner(lo, hi, body):
        lax.fori_loop(0, hi - lo, lambda t, c: (body(t + lo), c)[1], 0, unroll=UNROLL)

    def outer(lo, hi, reach, body):
        below = lo + reach
        above = B + reach - hi
        skip = EXT - B - 2 * reach

        def step(t, carry):
            body(wrap(t + hi + jnp.where(t >= above, skip, 0)))
            return carry
        lax.fori_loop(0, below + above, step, 0, unroll=True)

    def strain2(field, x, tiles=2):
        mid = [plane(field, c, x) for c in range(3)]
        dx = [along_x(field, c, x, tiles=tiles) for c in range(3)]
        dy = [along_y(f, tiles) for f in mid]
        dz = [along_z(f, tiles) for f in mid]
        return [
            (dx[0][t], dy[1][t], dz[2][t], dy[0][t] + dx[1][t], dz[0][t] + dx[2][t], dz[1][t] + dy[2][t])
            for t in range(tiles)
        ]

    def stress(field, S, E):
        def body(x):
            strains = strain2(field, x)
            k = lax.shift_right_logical(x, 2)
            for t, e in enumerate(strains):
                rows_t = pl.ds(B * t, B)
                hl, mu = PF[0, k, rows_t], PF[1, k, rows_t]
                common = hl * (e[0] + e[1] + e[2])
                hm = 0.5 * mu
                for c in range(3):
                    S[c, x, rows_t] = common + mu * e[c]
                    S[3 + c, x, rows_t] = hm * e[3 + c]
            for c in range(6):
                E[c, x] = strains[0][c]
        return body

    def force2(S, x, tiles=2):
        y = [along_y(plane(S, c, x), tiles) for c in (3, 1, 5)]
        z = [along_z(plane(S, c, x), tiles) for c in (4, 5, 2)]
        d = [along_x(S, c, x, tiles=tiles) for c in (0, 3, 4)]
        return [[d[c][t] + y[c][t] + z[c][t] for c in range(3)] for t in range(tiles)]

    def advance(x):
        for t, f in enumerate(force2(S0, x)):
            rows_t = pl.ds(B * t, B)
            push = PF[2, lax.shift_right_logical(x, 2), rows_t]
            for c in range(3):
                A1[c, x, rows_t] = A[c, x, rows_t] + V[c, x, rows_t] + push * (f[c] + Q[c, x, rows_t])

    def forward_strain(x):
        for n in range(steps):
            (f,) = strain2(F.at[n + 1], x, 1)
            for c in range(6):
                FS[n, c, x] = f[c]

    def acceleration(x):
        for n in range(steps):
            for c in range(3):
                AC[n, c, x] = F[n + 2, c, x, 0:B] - 2.0 * F[n + 1, c, x, 0:B] + F[n, c, x, 0:B]

    scale = 1.0 / math.sqrt(ratio**3 * steps * n_ev)

    def kernel_sums(field, E, n):
        def body(x):
            e = [E[c, x] for c in range(6)]
            f = [FS[n, c, x] for c in range(6)]
            both = (e[0] + e[1] + e[2]) * (f[0] + f[1] + f[2])
            pure = 2.0 * (e[0] * f[0] + e[1] * f[1] + e[2] * f[2]) + (e[3] * f[3] + e[4] * f[4] + e[5] * f[5])
            move = field[0, x, 0:B] * AC[n, 0, x] + field[1, x, 0:B] * AC[n, 1, x] + field[2, x, 0:B] * AC[n, 2, x]
            for m, (v, w) in enumerate(((both, 0.25), (pure, 0.25), (move, 1.0))):
                v = v * (w * scale)
                KX[m, x] = v if n == 0 else KX[m, x] + v
        return body

    local[1].wait()
    bytes_of(S0.at[:, pl.ds(0, 3 * EXT // 4)], lsem.at[0]).wait()
    inner(0, B, acceleration)
    arrived(0, False)
    arrived(1, False)
    constants(0)
    inner(1, B - 1, stress(A, S0, E0))
    arrived(2, False)
    inner(2, B - 2, advance)
    inner(3, B - 3, stress(A1, S1, E1))
    inner(1, B - 1, forward_strain)
    inner(1, B - 1, kernel_sums(A, E0, 0))
    inner(3, B - 3, kernel_sums(A1, E1, 1))

    arrived(0, True)
    constants(1)
    arrived(1, True)
    outer(1, B - 1, 3, stress(A, S0, E0))
    arrived(2, True)
    outer(2, B - 2, 2, advance)
    outer(3, B - 3, 1, stress(A1, S1, E1))
    outer(1, B - 1, 0, forward_strain)
    outer(1, B - 1, 0, kernel_sums(A, E0, 0))
    outer(3, B - 3, 0, kernel_sums(A1, E1, 1))

    sums = []
    for m in range(3):
        for k in range(B // ratio):
            v = sum(KX[m, ratio * k + j] for j in range(1, ratio)) + KX[m, ratio * k]
            v = v + pltpu.roll(v, B - 1, 0)
            sums.append(v + pltpu.roll(v, B - 2, 0))
    spot = lax.bitwise_and(sub, 3)
    halves = []
    for at in (0, 4):
        v = sums[at]
        for j in range(1, min(4, len(sums) - at)):
            v = jnp.where(spot == j, pltpu.roll(sums[at + j], j, 0), v)
        halves.append(v)
    wide = jnp.concatenate(halves, axis=1)
    wi = lax.broadcasted_iota(jnp.int32, (2 * depth, depth), 0)
    wj = lax.broadcasted_iota(jnp.int32, (2 * depth, depth), 1)
    T[...] = times_ones(wide, jnp.where(wi // ratio == wj, 1.0, 0.0))
    parts = [pltpu.make_async_remote_copy(
        src_ref=T, dst_ref=G.at[o - 1], send_sem=gsem.at[0], recv_sem=gsem.at[1],
        device_id={"event": lax.rem(ev + o, n_ev)}, device_id_type=MESH) for o in range(1, n_ev)]
    answered(2)
    for c in parts:
        c.start()

    def finish(x):
        (f,) = force2(S1, x, 1)
        push = PF[2, lax.shift_right_logical(x, 2), 0:B]
        for c in range(3):
            aend[0, c, x] = 2.0 * A1[c, x, 0:B] - A[c, x, 0:B] + push * (f[c] + Q[3 + c, x, 0:B])
    inner(0, B, finish)
    sent()
    bytes_of(G, gsem.at[0]).wait()
    bytes_of(G, gsem.at[1]).wait()
    total = T[...]
    for o in range(n_ev - 1):
        total = total + G[o]
    width = nzc // n_ev
    mine = pltpu.roll(total, lax.rem(depth - width * ev, depth), 1)
    other = pltpu.roll(mine, depth - nzc, 1)
    for m in range(3):
        for k in range(2):
            i = 2 * m + k
            src = mine if i < 4 else other
            for y in range(2):
                grad[m, k, y:y + 1] = src[4 * y + i % 4:4 * y + i % 4 + 1, 0:width]


def put_out(aend, grad, aend_out, grad_out, sems):
    copies = [pltpu.make_async_copy(aend, aend_out, sems.at[0]), pltpu.make_async_copy(grad, grad_out, sems.at[1])]
    for c in copies:
        c.start()
    for c in copies:
        c.wait()


def solution(mesh):
    n_gx, n_gy, n_ev = mesh.shape["gx"], mesh.shape["gy"], mesh.shape["event"]

    def on_device(adjoint, velocity, forward, receivers, residual, params):
        depth = adjoint.shape[-1]
        ratio = adjoint.shape[2] // params.shape[1]
        levels = forward.shape[1]
        steps = levels - 2
        nzc = params.shape[3]
        n_rec = receivers.shape[1]
        sizes = (n_gx, n_gy, n_ev, depth, ratio, steps)
        vm = pltpu.VMEM
        held = pl.pallas_call(
            functools.partial(kernel, sizes),
            out_shape=(
                pltpu.VMEM(adjoint.shape, F32),
                pltpu.VMEM((3, params.shape[1], params.shape[2], nzc // n_ev), F32),
            ),
            in_specs=[pl.BlockSpec(memory_space=pl.ANY)] * 6,
            out_specs=(pl.BlockSpec(memory_space=pltpu.VMEM), pl.BlockSpec(memory_space=pltpu.VMEM)),
            scratch_shapes=[
                vm((3, EXT, EXT, depth), F32),
                vm((3, EXT, EXT, depth), F32),
                vm((3, EXT, EXT, depth), F32),
                vm((levels, 3, EXT, EXT, depth), F32),
                vm((3, 4, 4, nzc), F32),
                vm((48, nzc), F32),
                vm((48, depth), F32),
                vm((3, 4, EXT, depth), F32),
                vm((1, n_rec), jnp.int32),
                vm((3, steps, n_rec), F32),
                vm((EXT * EXT, n_rec), BF16),
                vm((3 * steps, EXT, EXT, depth), F32),
                vm((6, EXT, EXT, depth), F32),
                vm((6, EXT, EXT, depth), F32),
                vm((6, EXT, B, depth), F32),
                vm((6, EXT, B, depth), F32),
                vm((steps, 6, B, B, depth), F32),
                vm((steps, 3, B, B, depth), F32),
                vm((3, B, B, depth), F32),
                vm((8, depth), F32),
                vm((n_ev - 1, 8, depth), F32),
                pltpu.SemaphoreType.DMA((4,)),
                pltpu.SemaphoreType.DMA((2, len(ORDER))),
                pltpu.SemaphoreType.DMA((2, len(ORDER))),
                pltpu.SemaphoreType.DMA((len(FACES),)),
                pltpu.SemaphoreType.DMA((2,)),
                pltpu.SemaphoreType.REGULAR((3,)),
            ],
            compiler_params=pltpu.CompilerParams(collective_id=0, has_side_effects=True),
        )(adjoint, velocity, forward, receivers, jnp.swapaxes(residual, 1, 2), params)
        return pl.pallas_call(
            put_out,
            out_shape=tuple(jax.ShapeDtypeStruct(h.shape, F32) for h in held),
            in_specs=[pl.BlockSpec(memory_space=pltpu.VMEM)] * 2,
            out_specs=(pl.BlockSpec(memory_space=pl.ANY),) * 2,
            scratch_shapes=[pltpu.SemaphoreType.DMA((2,))],
        )(*[pltpu.with_memory_space_constraint(h, pltpu.VMEM) for h in held])

    return jax.shard_map(
        on_device,
        mesh=mesh,
        in_specs=(
            P("event", None, "gx", "gy", None),
            P("event", None, "gx", "gy", None),
            P("event", None, None, "gx", "gy", None),
            P("event", None),
            P("event", None, None, None),
            P(None, "gx", "gy", None),
        ),
        out_specs=(P("event", None, "gx", "gy", None), P(None, "gx", "gy", "event")),
        check_vma=False,
    )
```

```python
import functools
import math

import jax
import jax.numpy as jnp
from jax import lax
from jax.experimental import pallas as pl
from jax.experimental.pallas import tpu as pltpu
from jax.sharding import PartitionSpec as P

STEP_DT2 = 0.1
MESH = pl.DeviceIdType.MESH
F32 = jnp.float32
BF16 = jnp.bfloat16
B = 8
EXT = 2 * B
UNROLL = 4
DIRS = [(dx, dy) for dx in (-1, 0, 1) for dy in (-1, 0, 1) if (dx, dy) != (0, 0)]
ORDER = sorted(DIRS, key=lambda d: (d[0] == 0, 0 in d))
FACES = [i for i, d in enumerate(ORDER) if 0 in d]


def span(d, w, own):
    if d == 0:
        return pl.ds(0, own), pl.ds(0, own)
    if d < 0:
        return pl.ds(0, w), pl.ds(own, w)
    return pl.ds(own - w, w), pl.ds(2 * own - w, w)


def times_ones(values, ones):
    pieces, left = [], values
    for _ in range(3):
        piece = left.astype(BF16)
        pieces.append(piece.astype(F32))
        left = left - pieces[-1]
    out = lax.dot_general(jnp.concatenate(pieces, axis=0).astype(BF16), ones.astype(BF16), (((1,), (0,)), ((), ())),
                          preferred_element_type=F32)
    n = values.shape[0]
    return out[0:n] + (out[n:2 * n] + out[2 * n:3 * n])


def kernel(sizes, adj, vel, fwd, rec, res, par, aend, grad,
           A, A1, V, F, C, C2, ZF, PF, REC, RES, OH, Q, S0, S1, E0, E1, FS, AC, KX, T, G,
           lsem, ssem, rsem, rsem_faces, gsem, gate):
    n_gx, n_gy, n_ev, depth, ratio, steps = sizes
    gx, gy, ev = lax.axis_index("gx"), lax.axis_index("gy"), lax.axis_index("event")
    has_x = {-1: gx > 0, 1: gx < n_gx - 1}
    has_y = {-1: gy > 0, 1: gy < n_gy - 1}

    def there(dx, dy):
        if dx == 0:
            return has_y[dy]
        if dy == 0:
            return has_x[dx]
        return jnp.logical_and(has_x[dx], has_y[dy])

    n_z, n_x = n_gx // 2, n_ev

    def late(v, n, step):
        return 13 * step * v + 800 * (v + (2 * v > n).astype(jnp.int32) * (n - 2 * v)), step * v

    def add(*terms):
        return sum(t[0] for t in terms), sum(t[1] for t in terms)

    def of_gx(px, pe):
        return add(late(lax.rem(px, n_z), n_z, 2 * n_x * n_gy), late((px // n_z) * (n_ev // 2) + pe // 2, n_x, 2))

    def of_core(pe):
        core = lax.rem(pe, 2)
        return -387 * core, core

    def turn(*terms):
        when, place = add(*terms)
        return (when + (place == 0).astype(jnp.int32) * 20000) * 2048 + place

    in_gx = {d: of_gx(gx + d, ev) for d in (-1, 0, 1)}
    in_gy = {d: late(gy + d, n_gy, 2 * n_x) for d in (-1, 0, 1)}
    core = of_core(ev)
    my_turn = turn(in_gx[0], in_gy[0], core)
    mates = []
    for dx, dy in ORDER:
        mates.append((there(dx, dy), turn(in_gx[dx], in_gy[dy], core) > my_turn, {"gx": gx + dx, "gy": gy + dy}))
    for o in range(1, n_ev):
        mate = lax.rem(ev + o, n_ev)
        mates.append((None, turn(of_gx(gx, mate), in_gy[0], of_core(mate)) > my_turn, {"event": mate}))
    later, earlier = [], []
    for exists, after, _ in mates:
        later.append(after if exists is None else jnp.logical_and(exists, after))
        before = jnp.logical_not(after)
        earlier.append(before if exists is None else jnp.logical_and(exists, before))

    barrier = pltpu.get_barrier_semaphore()
    for (_, _, device), cond in zip(mates, later):
        @pl.when(cond)
        def _(device=device):
            pl.semaphore_signal(barrier, inc=1, device_id=device, device_id_type=MESH)
    greetings = sum(c.astype(jnp.int32) for c in earlier)

    @pl.when(greetings > 0)
    def _():
        pl.semaphore_wait(barrier, greetings)

    own = pl.ds(0, B)
    local = [
        pltpu.make_async_copy(adj.at[0], A.at[:, own, own, :], lsem.at[0]),
        pltpu.make_async_copy(par, C.at[:, pl.ds(0, 2), pl.ds(0, 2), :], lsem.at[1]),
        pltpu.make_async_copy(vel.at[0], V.at[:, own, own, :], lsem.at[0]),
        pltpu.make_async_copy(fwd.at[0], F.at[:, :, own, own, :], lsem.at[0]),
        pltpu.make_async_copy(rec, REC, lsem.at[2]),
        pltpu.make_async_copy(res.at[0], RES, lsem.at[3]),
    ]

    def bytes_of(ref, sem):
        return pltpu.make_async_copy(ref, ref, sem)

    def messages(kind, i):
        dx, dy = ORDER[i]
        corner = dx != 0 and dy != 0
        pairs = []

        def layer(src, dst, wx, wy, size, at=0):
            (sx, tx), (sy, ty) = span(dx, wx, size), span(dy, wy, size)
            if at:
                sx = pl.ds(size - at if dx > 0 else at - 1, 1)
                tx = pl.ds(2 * size - at if dx > 0 else size + at - 1, 1)
            pairs.append((src(sx, sy), dst(tx, ty)))

        if kind == 0:
            layer(lambda x, y: par.at[:, x, y, :], lambda x, y: C.at[:, x, y, :], 1, 1, 2)
        elif kind == 1 and corner:
            for at in (1, 2, 3):
                layer(lambda x, y: adj.at[0, :, x, y, :], lambda x, y: A.at[:, x, y, :], 1, 4 - at, B, at)
            layer(lambda x, y: vel.at[0, :, x, y, :], lambda x, y: V.at[:, x, y, :], 1, 1, B)
        elif kind == 1:
            layer(lambda x, y: adj.at[0, :, x, y, :], lambda x, y: A.at[:, x, y, :], 4, 4, B)
        elif kind == 2:
            layer(lambda x, y: vel.at[0, :, x, y, :], lambda x, y: V.at[:, x, y, :], 2, 2, B)
        else:
            levels = pl.ds(1, steps)
            layer(lambda x, y: fwd.at[0, levels, :, x, y, :], lambda x, y: F.at[levels, :, x, y, :], 1, 1, B)
        send_sem = ssem.at[0 if kind == 0 else 1, i]
        recv_sem = rsem_faces.at[kind - 2, FACES.index(i)] if kind >= 2 else rsem.at[kind, i]
        return [pltpu.make_async_remote_copy(
            src_ref=src, dst_ref=dst, send_sem=send_sem, recv_sem=recv_sem,
            device_id={"gx": gx + dx, "gy": gy + dy}, device_id_type=MESH) for src, dst in pairs]

    def wait_rows(n, sem):
        bytes_of(A1.at[:, pl.ds(0, n // B), pl.ds(0, B)] if n % B == 0 else A1.at[:, pl.ds(0, 1), pl.ds(0, n)], sem).wait()

    def send(kind, i, cond):
        @pl.when(cond)
        def _():
            for m in messages(kind, i):
                m.start()

    def sent():
        for i, d in enumerate(ORDER):
            @pl.when(there(*d))
            def _(i=i, d=d):
                messages(0, i)[0].wait_send()
                wait_rows(7 if 0 not in d else (6 + steps) * B, ssem.at[1, i])

    def arrived(kind, from_x):
        for i, (dx, dy) in enumerate(ORDER):
            corner = dx != 0 and dy != 0
            if (dx != 0) != from_x or (kind >= 2 and corner):
                continue

            @pl.when(there(-dx, -dy))
            def _(i=i, corner=corner):
                if kind == 0:
                    messages(0, i)[0].wait_recv()
                elif kind == 1:
                    wait_rows(7 if corner else 4 * B, rsem.at[1, i])
                else:
                    wait_rows((2 if kind == 2 else steps) * B, rsem_faces.at[kind - 2, FACES.index(i)])

    def group(i):
        return 2 if i >= len(ORDER) else 3 if 0 not in ORDER[i] else int(ORDER[i][0] != 0)

    def answered(which):
        n = sum(c.astype(jnp.int32) for i, c in enumerate(later) if group(i) == which)

        @pl.when(n > 0)
        def _():
            pl.semaphore_wait(gate.at[which], n)

    def send_after_answer(which):
        answered(which)
        for kind in range(4):
            for i in range(len(ORDER)):
                if group(i) == which and (kind < 2 or 0 in ORDER[i]):
                    send(kind, i, later[i])

    for kind in (0, 1):
        for i in range(len(ORDER)):
            send(kind, i, earlier[i])
    for i, ((_, _, device), cond) in enumerate(zip(mates, earlier)):
        @pl.when(cond)
        def _(device=device, which=group(i)):
            pl.semaphore_signal(gate.at[which], inc=1, device_id=device, device_id_type=MESH)
    def send_rest(which):
        for kind in (2, 3):
            for i in FACES:
                if group(i) == which:
                    send(kind, i, earlier[i])

    send_rest(0)
    for c in local:
        c.start()

    for d in (-1, 1):
        lo = B + B // 2 if d < 0 else B
        cl = 3 if d < 0 else 2
        x_fill, y_fill = pl.ds(lo, B // 2), pl.ds(lo, B // 2)

        @pl.when(jnp.logical_not(has_x[d]))
        def _(x_fill=x_fill, cl=cl, lo=lo, d=d):
            A[:, x_fill] = jnp.zeros((3, B // 2, EXT, depth), F32)
            V[:, x_fill] = jnp.zeros((3, B // 2, EXT, depth), F32)
            fx = EXT - 1 if d < 0 else B
            for t in range(1, steps + 1):
                F[t, :, fx] = jnp.zeros((3, EXT, depth), F32)
            C[:, cl] = jnp.zeros((3, 4, C.shape[3]), F32)

        @pl.when(jnp.logical_not(has_y[d]))
        def _(y_fill=y_fill, cl=cl):
            A[:, :, y_fill] = jnp.zeros((3, EXT, B // 2, depth), F32)
            V[:, :, y_fill] = jnp.zeros((3, EXT, B // 2, depth), F32)
            for t in range(1, steps + 1):
                F[t, :, :, y_fill] = jnp.zeros((3, EXT, B // 2, depth), F32)
            C[:, :, pl.ds(cl, 1)] = jnp.zeros((3, 4, 1, C.shape[3]), F32)

    local[4].wait()
    local[5].wait()
    cells = REC[...]
    all_y = B * n_gy
    cz = lax.bitwise_and(cells, depth - 1)
    cy = lax.bitwise_and(lax.shift_right_logical(cells, int(math.log2(depth))), all_y - 1)
    cx = lax.shift_right_logical(cells, int(math.log2(depth * all_y)))
    lx, ly = cx - gx * B, cy - gy * B
    half = B // 2
    near = (lx >= -half) & (lx < B + half) & (ly >= -half) & (ly < B + half)
    place = jnp.where(near, lax.bitwise_and(lx, EXT - 1) * EXT + lax.bitwise_and(ly, EXT - 1), -1)
    n_rec = cells.shape[1]
    rows = lax.broadcasted_iota(jnp.int32, (EXT * EXT, n_rec), 0)
    OH[...] = jnp.where(rows == place, 1.0, 0.0).astype(BF16)
    at_z = lax.broadcasted_iota(jnp.int32, (depth, n_rec), 0) == cz

    for n in range(steps):
        for c in range(3):
            left = 2.0 * RES[c, n:n + 1, :]
            spread = jnp.zeros((EXT * EXT, depth), F32)
            for _ in range(3):
                piece = left.astype(BF16).astype(F32)
                left = left - piece
                b = jnp.where(at_z, piece, 0.0).astype(BF16)
                spread = spread + lax.dot_general(OH[...], b, (((1,), (1,)), ((), ())), preferred_element_type=F32)
            Q[3 * n + c] = spread.reshape(EXT, EXT, depth)

    send_rest(1)
    send_after_answer(0)
    send_after_answer(1)

    nzc = C.shape[3]
    zi = lax.broadcasted_iota(jnp.int32, (nzc, depth), 0)
    zj = lax.broadcasted_iota(jnp.int32, (nzc, depth), 1)
    widen = jnp.where(zi == zj // ratio, 1.0, 0.0)
    row = lax.broadcasted_iota(jnp.int32, (EXT, depth), 0)

    def constants(part):
        for k in range(2 * part, 2 * part + 2):
            for p in range(3):
                C2[pl.ds(12 * k + 4 * p, 4), :] = C[p, k]
        here = pl.ds(24 * part, 24)
        ZF[here] = times_ones(C2[here], widen)
        for k in range(2 * part, 2 * part + 2):
            for p in range(3):
                r = [ZF[pl.ds(12 * k + 4 * p + j, 1), :] for j in range(4)]
                fine = jnp.where(row < 4, r[0], jnp.where(row < 8, r[1], jnp.where(row < 12, r[2], r[3])))
                if p == 0:
                    PF[0, k] = 0.5 * fine
                elif p == 1:
                    PF[1, k] = fine
                else:
                    outside = fine == 0.0
                    PF[2, k] = jnp.where(outside, 0.0, (0.5 * STEP_DT2) / jnp.where(outside, 1.0, fine))

    lane = lax.broadcasted_iota(jnp.int32, (B, depth), 1)
    not_last, not_first = lane < depth - 1, lane > 0
    sub = lax.broadcasted_iota(jnp.int32, (B, depth), 0)
    at_top, at_end = sub == 0, sub == B - 1

    def plane(ref, *at, tiles=2):
        return [ref[(*at, pl.ds(B * t, B))] for t in range(tiles)]

    def along_y(f, tiles=2):
        out = []
        for t in range(tiles):
            a, b = f[t], f[1 - t]
            out.append(pltpu.roll(jnp.where(at_top, b, a), B - 1, 0) - pltpu.roll(jnp.where(at_end, b, a), 1, 0))
        return out

    def along_z(f, tiles=2):
        return [
            jnp.where(not_last, pltpu.roll(g, depth - 1, 1), 0.0) - jnp.where(not_first, pltpu.roll(g, 1, 1), 0.0)
            for g in f[:tiles]
        ]

    def along_x(ref, *at, tiles=2):
        *at, x = at
        up, down = plane(ref, *at, wrap(x + 1), tiles=tiles), plane(ref, *at, wrap(x - 1), tiles=tiles)
        return [a - b for a, b in zip(up, down)]

    def wrap(x):
        return lax.bitwise_and(x, EXT - 1)

    def inner(lo, hi, body):
        lax.fori_loop(0, hi - lo, lambda t, c: (body(t + lo), c)[1], 0, unroll=UNROLL)

    def outer(lo, hi, reach, body):
        below = lo + reach
        above = B + reach - hi
        skip = EXT - B - 2 * reach

        def step(t, carry):
            body(wrap(t + hi + jnp.where(t >= above, skip, 0)))
            return carry
        lax.fori_loop(0, below + above, step, 0, unroll=True)

    def strain2(field, x, tiles=2):
        mid = [plane(field, c, x) for c in range(3)]
        dx = [along_x(field, c, x, tiles=tiles) for c in range(3)]
        dy = [along_y(f, tiles) for f in mid]
        dz = [along_z(f, tiles) for f in mid]
        return [
            (dx[0][t], dy[1][t], dz[2][t], dy[0][t] + dx[1][t], dz[0][t] + dx[2][t], dz[1][t] + dy[2][t])
            for t in range(tiles)
        ]

    def stress(field, S, E):
        def body(x):
            strains = strain2(field, x)
            k = lax.shift_right_logical(x, 2)
            for t, e in enumerate(strains):
                rows_t = pl.ds(B * t, B)
                hl, mu = PF[0, k, rows_t], PF[1, k, rows_t]
                common = hl * (e[0] + e[1] + e[2])
                hm = 0.5 * mu
                for c in range(3):
                    S[c, x, rows_t] = common + mu * e[c]
                    S[3 + c, x, rows_t] = hm * e[3 + c]
            for c in range(6):
                E[c, x] = strains[0][c]
        return body

    def force2(S, x, tiles=2):
        y = [along_y(plane(S, c, x), tiles) for c in (3, 1, 5)]
        z = [along_z(plane(S, c, x), tiles) for c in (4, 5, 2)]
        d = [along_x(S, c, x, tiles=tiles) for c in (0, 3, 4)]
        return [[d[c][t] + y[c][t] + z[c][t] for c in range(3)] for t in range(tiles)]

    def advance(x):
        for t, f in enumerate(force2(S0, x)):
            rows_t = pl.ds(B * t, B)
            push = PF[2, lax.shift_right_logical(x, 2), rows_t]
            for c in range(3):
                A1[c, x, rows_t] = A[c, x, rows_t] + V[c, x, rows_t] + push * (f[c] + Q[c, x, rows_t])

    def forward_strain(x):
        for n in range(steps):
            (f,) = strain2(F.at[n + 1], x, 1)
            for c in range(6):
                FS[n, c, x] = f[c]

    def acceleration(x):
        for n in range(steps):
            for c in range(3):
                AC[n, c, x] = F[n + 2, c, x, 0:B] - 2.0 * F[n + 1, c, x, 0:B] + F[n, c, x, 0:B]

    scale = 1.0 / math.sqrt(ratio**3 * steps * n_ev)

    def kernel_sums(field, E, n):
        def body(x):
            e = [E[c, x] for c in range(6)]
            f = [FS[n, c, x] for c in range(6)]
            both = (e[0] + e[1] + e[2]) * (f[0] + f[1] + f[2])
            pure = 2.0 * (e[0] * f[0] + e[1] * f[1] + e[2] * f[2]) + (e[3] * f[3] + e[4] * f[4] + e[5] * f[5])
            move = field[0, x, 0:B] * AC[n, 0, x] + field[1, x, 0:B] * AC[n, 1, x] + field[2, x, 0:B] * AC[n, 2, x]
            for m, (v, w) in enumerate(((both, 0.25), (pure, 0.25), (move, 1.0))):
                v = v * (w * scale)
                KX[m, x] = v if n == 0 else KX[m, x] + v
        return body

    local[1].wait()
    bytes_of(S0.at[:, pl.ds(0, 3 * EXT // 4)], lsem.at[0]).wait()
    inner(0, B, acceleration)
    arrived(0, False)
    arrived(1, False)
    constants(0)
    inner(1, B - 1, stress(A, S0, E0))
    arrived(2, False)
    inner(2, B - 2, advance)
    inner(3, B - 3, stress(A1, S1, E1))
    arrived(3, False)
    inner(1, B - 1, forward_strain)
    inner(1, B - 1, kernel_sums(A, E0, 0))
    inner(3, B - 3, kernel_sums(A1, E1, 1))

    send_after_answer(3)

    arrived(0, True)
    constants(1)
    arrived(1, True)
    outer(1, B - 1, 3, stress(A, S0, E0))
    arrived(2, True)
    outer(2, B - 2, 2, advance)
    outer(3, B - 3, 1, stress(A1, S1, E1))
    arrived(3, True)
    outer(1, B - 1, 0, forward_strain)
    outer(1, B - 1, 0, kernel_sums(A, E0, 0))
    outer(3, B - 3, 0, kernel_sums(A1, E1, 1))

    sums = []
    for m in range(3):
        for k in range(B // ratio):
            v = sum(KX[m, ratio * k + j] for j in range(1, ratio)) + KX[m, ratio * k]
            v = v + pltpu.roll(v, B - 1, 0)
            sums.append(v + pltpu.roll(v, B - 2, 0))
    spot = lax.bitwise_and(sub, 3)
    halves = []
    for at in (0, 4):
        v = sums[at]
        for j in range(1, min(4, len(sums) - at)):
            v = jnp.where(spot == j, pltpu.roll(sums[at + j], j, 0), v)
        halves.append(v)
    wide = jnp.concatenate(halves, axis=1)
    wi = lax.broadcasted_iota(jnp.int32, (2 * depth, depth), 0)
    wj = lax.broadcasted_iota(jnp.int32, (2 * depth, depth), 1)
    T[...] = times_ones(wide, jnp.where(wi // ratio == wj, 1.0, 0.0))
    parts = [pltpu.make_async_remote_copy(
        src_ref=T, dst_ref=G.at[o - 1], send_sem=gsem.at[0], recv_sem=gsem.at[1],
        device_id={"event": lax.rem(ev + o, n_ev)}, device_id_type=MESH) for o in range(1, n_ev)]
    answered(2)
    for c in parts:
        c.start()

    def finish(x):
        (f,) = force2(S1, x, 1)
        push = PF[2, lax.shift_right_logical(x, 2), 0:B]
        for c in range(3):
            aend[0, c, x] = 2.0 * A1[c, x, 0:B] - A[c, x, 0:B] + push * (f[c] + Q[3 + c, x, 0:B])
    inner(0, B, finish)
    sent()
    bytes_of(G, gsem.at[0]).wait()
    bytes_of(G, gsem.at[1]).wait()
    total = T[...]
    for o in range(n_ev - 1):
        total = total + G[o]
    width = nzc // n_ev
    mine = pltpu.roll(total, lax.rem(depth - width * ev, depth), 1)
    other = pltpu.roll(mine, depth - nzc, 1)
    for m in range(3):
        for k in range(2):
            i = 2 * m + k
            src = mine if i < 4 else other
            for y in range(2):
                grad[m, k, y:y + 1] = src[4 * y + i % 4:4 * y + i % 4 + 1, 0:width]


def put_out(aend, grad, aend_out, grad_out, sems):
    copies = [pltpu.make_async_copy(aend, aend_out, sems.at[0]), pltpu.make_async_copy(grad, grad_out, sems.at[1])]
    for c in copies:
        c.start()
    for c in copies:
        c.wait()


def solution(mesh):
    n_gx, n_gy, n_ev = mesh.shape["gx"], mesh.shape["gy"], mesh.shape["event"]

    def on_device(adjoint, velocity, forward, receivers, residual, params):
        depth = adjoint.shape[-1]
        ratio = adjoint.shape[2] // params.shape[1]
        levels = forward.shape[1]
        steps = levels - 2
        nzc = params.shape[3]
        n_rec = receivers.shape[1]
        sizes = (n_gx, n_gy, n_ev, depth, ratio, steps)
        vm = pltpu.VMEM
        held = pl.pallas_call(
            functools.partial(kernel, sizes),
            out_shape=(
                pltpu.VMEM(adjoint.shape, F32),
                pltpu.VMEM((3, params.shape[1], params.shape[2], nzc // n_ev), F32),
            ),
            in_specs=[pl.BlockSpec(memory_space=pl.ANY)] * 6,
            out_specs=(pl.BlockSpec(memory_space=pltpu.VMEM), pl.BlockSpec(memory_space=pltpu.VMEM)),
            scratch_shapes=[
                vm((3, EXT, EXT, depth), F32),
                vm((3, EXT, EXT, depth), F32),
                vm((3, EXT, EXT, depth), F32),
                vm((levels, 3, EXT, EXT, depth), F32),
                vm((3, 4, 4, nzc), F32),
                vm((48, nzc), F32),
                vm((48, depth), F32),
                vm((3, 4, EXT, depth), F32),
                vm((1, n_rec), jnp.int32),
                vm((3, steps, n_rec), F32),
                vm((EXT * EXT, n_rec), BF16),
                vm((3 * steps, EXT, EXT, depth), F32),
                vm((6, EXT, EXT, depth), F32),
                vm((6, EXT, EXT, depth), F32),
                vm((6, EXT, B, depth), F32),
                vm((6, EXT, B, depth), F32),
                vm((steps, 6, B, B, depth), F32),
                vm((steps, 3, B, B, depth), F32),
                vm((3, B, B, depth), F32),
                vm((8, depth), F32),
                vm((n_ev - 1, 8, depth), F32),
                pltpu.SemaphoreType.DMA((4,)),
                pltpu.SemaphoreType.DMA((2, len(ORDER))),
                pltpu.SemaphoreType.DMA((2, len(ORDER))),
                pltpu.SemaphoreType.DMA((2, len(FACES))),
                pltpu.SemaphoreType.DMA((2,)),
                pltpu.SemaphoreType.REGULAR((4,)),
            ],
            compiler_params=pltpu.CompilerParams(collective_id=0, has_side_effects=True),
        )(adjoint, velocity, forward, receivers, jnp.swapaxes(residual, 1, 2), params)
        return pl.pallas_call(
            put_out,
            out_shape=tuple(jax.ShapeDtypeStruct(h.shape, F32) for h in held),
            in_specs=[pl.BlockSpec(memory_space=pltpu.VMEM)] * 2,
            out_specs=(pl.BlockSpec(memory_space=pl.ANY),) * 2,
            scratch_shapes=[pltpu.SemaphoreType.DMA((2,))],
        )(*[pltpu.with_memory_space_constraint(h, pltpu.VMEM) for h in held])

    return jax.shard_map(
        on_device,
        mesh=mesh,
        in_specs=(
            P("event", None, "gx", "gy", None),
            P("event", None, "gx", "gy", None),
            P("event", None, None, "gx", "gy", None),
            P("event", None),
            P("event", None, None, None),
            P(None, "gx", "gy", None),
        ),
        out_specs=(P("event", None, "gx", "gy", None), P(None, "gx", "gy", "event")),
        check_vma=False,
    )
```

```python
import functools
import math

import jax
import jax.numpy as jnp
from jax import lax
from jax.experimental import pallas as pl
from jax.experimental.pallas import tpu as pltpu
from jax.sharding import PartitionSpec as P

STEP_DT2 = 0.1
MESH = pl.DeviceIdType.MESH
F32 = jnp.float32
BF16 = jnp.bfloat16
B = 8
EXT = 2 * B
UNROLL = 4
DIRS = [(dx, dy) for dx in (-1, 0, 1) for dy in (-1, 0, 1) if (dx, dy) != (0, 0)]
ORDER = sorted(DIRS, key=lambda d: (d[0] == 0, 0 in d))
FACES = [i for i, d in enumerate(ORDER) if 0 in d]


def span(d, w, own):
    if d == 0:
        return pl.ds(0, own), pl.ds(0, own)
    if d < 0:
        return pl.ds(0, w), pl.ds(own, w)
    return pl.ds(own - w, w), pl.ds(2 * own - w, w)


def times_ones(values, ones):
    pieces, left = [], values
    for _ in range(3):
        piece = left.astype(BF16)
        pieces.append(piece.astype(F32))
        left = left - pieces[-1]
    out = lax.dot_general(jnp.concatenate(pieces, axis=0).astype(BF16), ones.astype(BF16), (((1,), (0,)), ((), ())),
                          preferred_element_type=F32)
    n = values.shape[0]
    return out[0:n] + (out[n:2 * n] + out[2 * n:3 * n])


def kernel(sizes, adj, vel, fwd, rec, res, par, aend, grad,
           A, A1, V, F, C, C2, ZF, PF, REC, RES, OH, Q, S0, S1, E0, E1, FS, AC, KX, T, G,
           lsem, ssem, rsem, rsem_faces, gsem, gate):
    n_gx, n_gy, n_ev, depth, ratio, steps = sizes
    gx, gy, ev = lax.axis_index("gx"), lax.axis_index("gy"), lax.axis_index("event")
    has_x = {-1: gx > 0, 1: gx < n_gx - 1}
    has_y = {-1: gy > 0, 1: gy < n_gy - 1}

    def there(dx, dy):
        if dx == 0:
            return has_y[dy]
        if dy == 0:
            return has_x[dx]
        return jnp.logical_and(has_x[dx], has_y[dy])

    n_z, n_x = n_gx // 2, n_ev

    def late(v, n, step):
        return 13 * step * v + 800 * (v + (2 * v > n).astype(jnp.int32) * (n - 2 * v)), step * v

    def add(*terms):
        return sum(t[0] for t in terms), sum(t[1] for t in terms)

    def of_gx(px, pe):
        return add(late(lax.rem(px, n_z), n_z, 2 * n_x * n_gy), late((px // n_z) * (n_ev // 2) + pe // 2, n_x, 2))

    def of_core(pe):
        core = lax.rem(pe, 2)
        return -387 * core, core

    def turn(*terms):
        when, place = add(*terms)
        return (when + (place == 0).astype(jnp.int32) * 20000) * 2048 + place

    in_gx = {d: of_gx(gx + d, ev) for d in (-1, 0, 1)}
    in_gy = {d: late(gy + d, n_gy, 2 * n_x) for d in (-1, 0, 1)}
    core = of_core(ev)
    my_turn = turn(in_gx[0], in_gy[0], core)
    mates = []
    for dx, dy in ORDER:
        mates.append((there(dx, dy), turn(in_gx[dx], in_gy[dy], core) > my_turn, {"gx": gx + dx, "gy": gy + dy}))
    for o in range(1, n_ev):
        mate = lax.rem(ev + o, n_ev)
        mates.append((None, turn(of_gx(gx, mate), in_gy[0], of_core(mate)) > my_turn, {"event": mate}))
    later, earlier = [], []
    for exists, after, _ in mates:
        later.append(after if exists is None else jnp.logical_and(exists, after))
        before = jnp.logical_not(after)
        earlier.append(before if exists is None else jnp.logical_and(exists, before))

    barrier = pltpu.get_barrier_semaphore()
    for (_, _, device), cond in zip(mates, later):
        @pl.when(cond)
        def _(device=device):
            pl.semaphore_signal(barrier, inc=1, device_id=device, device_id_type=MESH)
    greetings = sum(c.astype(jnp.int32) for c in earlier)

    @pl.when(greetings > 0)
    def _():
        pl.semaphore_wait(barrier, greetings)

    own = pl.ds(0, B)
    local = [
        pltpu.make_async_copy(adj.at[0], A.at[:, own, own, :], lsem.at[0]),
        pltpu.make_async_copy(par, C.at[:, pl.ds(0, 2), pl.ds(0, 2), :], lsem.at[1]),
        pltpu.make_async_copy(vel.at[0], V.at[:, own, own, :], lsem.at[0]),
        pltpu.make_async_copy(fwd.at[0], F.at[:, :, own, own, :], lsem.at[0]),
        pltpu.make_async_copy(rec, REC, lsem.at[2]),
        pltpu.make_async_copy(res.at[0], RES, lsem.at[3]),
    ]

    def bytes_of(ref, sem):
        return pltpu.make_async_copy(ref, ref, sem)

    def messages(kind, i):
        dx, dy = ORDER[i]
        corner = dx != 0 and dy != 0
        pairs = []

        def layer(src, dst, wx, wy, size, at=0):
            (sx, tx), (sy, ty) = span(dx, wx, size), span(dy, wy, size)
            if at:
                sx = pl.ds(size - at if dx > 0 else at - 1, 1)
                tx = pl.ds(2 * size - at if dx > 0 else size + at - 1, 1)
            pairs.append((src(sx, sy), dst(tx, ty)))

        if kind == 0:
            layer(lambda x, y: par.at[:, x, y, :], lambda x, y: C.at[:, x, y, :], 1, 1, 2)
        elif kind == 1 and corner:
            for at in (1, 2, 3):
                layer(lambda x, y: adj.at[0, :, x, y, :], lambda x, y: A.at[:, x, y, :], 1, 4 - at, B, at)
            layer(lambda x, y: vel.at[0, :, x, y, :], lambda x, y: V.at[:, x, y, :], 1, 1, B)
        elif kind == 1:
            layer(lambda x, y: adj.at[0, :, x, y, :], lambda x, y: A.at[:, x, y, :], 4, 4, B)
        elif kind == 2:
            layer(lambda x, y: vel.at[0, :, x, y, :], lambda x, y: V.at[:, x, y, :], 2, 2, B)
        else:
            levels = pl.ds(1, steps)
            layer(lambda x, y: fwd.at[0, levels, :, x, y, :], lambda x, y: F.at[levels, :, x, y, :], 1, 1, B)
        send_sem = ssem.at[0 if kind == 0 else 1, i]
        recv_sem = rsem_faces.at[kind - 2, FACES.index(i)] if kind >= 2 else rsem.at[kind, i]
        return [pltpu.make_async_remote_copy(
            src_ref=src, dst_ref=dst, send_sem=send_sem, recv_sem=recv_sem,
            device_id={"gx": gx + dx, "gy": gy + dy}, device_id_type=MESH) for src, dst in pairs]

    def wait_rows(n, sem):
        bytes_of(A1.at[:, pl.ds(0, n // B), pl.ds(0, B)] if n % B == 0 else A1.at[:, pl.ds(0, 1), pl.ds(0, n)], sem).wait()

    def send(kind, i, cond):
        @pl.when(cond)
        def _():
            for m in messages(kind, i):
                m.start()

    def sent():
        for i, d in enumerate(ORDER):
            @pl.when(there(*d))
            def _(i=i, d=d):
                messages(0, i)[0].wait_send()
                wait_rows(7 if 0 not in d else (6 + steps) * B, ssem.at[1, i])

    def arrived(kind, from_x):
        for i, (dx, dy) in enumerate(ORDER):
            corner = dx != 0 and dy != 0
            if (dx != 0) != from_x or (kind >= 2 and corner):
                continue

            @pl.when(there(-dx, -dy))
            def _(i=i, corner=corner):
                if kind == 0:
                    messages(0, i)[0].wait_recv()
                elif kind == 1:
                    wait_rows(7 if corner else 4 * B, rsem.at[1, i])
                else:
                    wait_rows((2 if kind == 2 else steps) * B, rsem_faces.at[kind - 2, FACES.index(i)])

    def group(i):
        return 2 if i >= len(ORDER) else 3 if 0 not in ORDER[i] else int(ORDER[i][0] != 0)

    def answered(which):
        n = sum(c.astype(jnp.int32) for i, c in enumerate(later) if group(i) == which)

        @pl.when(n > 0)
        def _():
            pl.semaphore_wait(gate.at[which], n)

    def send_after_answer(which):
        answered(which)
        for kind in range(4):
            for i in range(len(ORDER)):
                if group(i) == which and (kind < 2 or 0 in ORDER[i]):
                    send(kind, i, later[i])

    for kind in (0, 1):
        for i in range(len(ORDER)):
            send(kind, i, earlier[i])
    for i, ((_, _, device), cond) in enumerate(zip(mates, earlier)):
        @pl.when(cond)
        def _(device=device, which=group(i)):
            pl.semaphore_signal(gate.at[which], inc=1, device_id=device, device_id_type=MESH)
    def send_rest(which):
        for kind in (2, 3):
            for i in FACES:
                if group(i) == which:
                    send(kind, i, earlier[i])

    send_rest(0)
    for c in local:
        c.start()

    for d in (-1, 1):
        lo = B + B // 2 if d < 0 else B
        cl = 3 if d < 0 else 2
        x_fill, y_fill = pl.ds(lo, B // 2), pl.ds(lo, B // 2)

        @pl.when(jnp.logical_not(has_x[d]))
        def _(x_fill=x_fill, cl=cl, lo=lo, d=d):
            A[:, x_fill] = jnp.zeros((3, B // 2, EXT, depth), F32)
            V[:, x_fill] = jnp.zeros((3, B // 2, EXT, depth), F32)
            fx = EXT - 1 if d < 0 else B
            for t in range(1, steps + 1):
                F[t, :, fx] = jnp.zeros((3, EXT, depth), F32)
            C[:, cl] = jnp.zeros((3, 4, C.shape[3]), F32)

        @pl.when(jnp.logical_not(has_y[d]))
        def _(y_fill=y_fill, cl=cl):
            A[:, :, y_fill] = jnp.zeros((3, EXT, B // 2, depth), F32)
            V[:, :, y_fill] = jnp.zeros((3, EXT, B // 2, depth), F32)
            for t in range(1, steps + 1):
                F[t, :, :, y_fill] = jnp.zeros((3, EXT, B // 2, depth), F32)
            C[:, :, pl.ds(cl, 1)] = jnp.zeros((3, 4, 1, C.shape[3]), F32)

    local[4].wait()
    local[5].wait()
    cells = REC[...]
    all_y = B * n_gy
    cz = lax.bitwise_and(cells, depth - 1)
    cy = lax.bitwise_and(lax.shift_right_logical(cells, int(math.log2(depth))), all_y - 1)
    cx = lax.shift_right_logical(cells, int(math.log2(depth * all_y)))
    lx, ly = cx - gx * B, cy - gy * B
    half = B // 2
    near = (lx >= -half) & (lx < B + half) & (ly >= -half) & (ly < B + half)
    place = jnp.where(near, lax.bitwise_and(lx, EXT - 1) * EXT + lax.bitwise_and(ly, EXT - 1), -1)
    n_rec = cells.shape[1]
    rows = lax.broadcasted_iota(jnp.int32, (EXT * EXT, n_rec), 0)
    OH[...] = jnp.where(rows == place, 1.0, 0.0).astype(BF16)
    at_z = lax.broadcasted_iota(jnp.int32, (depth, n_rec), 0) == cz

    for n in range(steps):
        for c in range(3):
            left = 2.0 * RES[c, n:n + 1, :]
            spread = jnp.zeros((EXT * EXT, depth), F32)
            for _ in range(3):
                piece = left.astype(BF16).astype(F32)
                left = left - piece
                b = jnp.where(at_z, piece, 0.0).astype(BF16)
                spread = spread + lax.dot_general(OH[...], b, (((1,), (1,)), ((), ())), preferred_element_type=F32)
            Q[3 * n + c] = spread.reshape(EXT, EXT, depth)
        if n == 0:
            send_rest(1)

    send_after_answer(0)
    send_after_answer(1)

    nzc = C.shape[3]
    zi = lax.broadcasted_iota(jnp.int32, (nzc, depth), 0)
    zj = lax.broadcasted_iota(jnp.int32, (nzc, depth), 1)
    widen = jnp.where(zi == zj // ratio, 1.0, 0.0)
    row = lax.broadcasted_iota(jnp.int32, (EXT, depth), 0)

    def constants(part):
        for k in range(2 * part, 2 * part + 2):
            for p in range(3):
                C2[pl.ds(12 * k + 4 * p, 4), :] = C[p, k]
        here = pl.ds(24 * part, 24)
        ZF[here] = times_ones(C2[here], widen)
        for k in range(2 * part, 2 * part + 2):
            for p in range(3):
                r = [ZF[pl.ds(12 * k + 4 * p + j, 1), :] for j in range(4)]
                fine = jnp.where(row < 4, r[0], jnp.where(row < 8, r[1], jnp.where(row < 12, r[2], r[3])))
                if p == 0:
                    PF[0, k] = 0.5 * fine
                elif p == 1:
                    PF[1, k] = fine
                else:
                    outside = fine == 0.0
                    PF[2, k] = jnp.where(outside, 0.0, (0.5 * STEP_DT2) / jnp.where(outside, 1.0, fine))

    lane = lax.broadcasted_iota(jnp.int32, (B, depth), 1)
    not_last, not_first = lane < depth - 1, lane > 0
    sub = lax.broadcasted_iota(jnp.int32, (B, depth), 0)
    at_top, at_end = sub == 0, sub == B - 1

    def plane(ref, *at, tiles=2):
        return [ref[(*at, pl.ds(B * t, B))] for t in range(tiles)]

    def along_y(f, tiles=2):
        out = []
        for t in range(tiles):
            a, b = f[t], f[1 - t]
            out.append(pltpu.roll(jnp.where(at_top, b, a), B - 1, 0) - pltpu.roll(jnp.where(at_end, b, a), 1, 0))
        return out

    def along_z(f, tiles=2):
        return [
            jnp.where(not_last, pltpu.roll(g, depth - 1, 1), 0.0) - jnp.where(not_first, pltpu.roll(g, 1, 1), 0.0)
            for g in f[:tiles]
        ]

    def along_x(ref, *at, tiles=2):
        *at, x = at
        up, down = plane(ref, *at, wrap(x + 1), tiles=tiles), plane(ref, *at, wrap(x - 1), tiles=tiles)
        return [a - b for a, b in zip(up, down)]

    def wrap(x):
        return lax.bitwise_and(x, EXT - 1)

    def inner(lo, hi, body):
        lax.fori_loop(0, hi - lo, lambda t, c: (body(t + lo), c)[1], 0, unroll=UNROLL)

    def outer(lo, hi, reach, body):
        below = lo + reach
        above = B + reach - hi
        skip = EXT - B - 2 * reach

        def step(t, carry):
            body(wrap(t + hi + jnp.where(t >= above, skip, 0)))
            return carry
        lax.fori_loop(0, below + above, step, 0, unroll=True)

    def strain2(field, x, tiles=2):
        mid = [plane(field, c, x) for c in range(3)]
        dx = [along_x(field, c, x, tiles=tiles) for c in range(3)]
        dy = [along_y(f, tiles) for f in mid]
        dz = [along_z(f, tiles) for f in mid]
        return [
            (dx[0][t], dy[1][t], dz[2][t], dy[0][t] + dx[1][t], dz[0][t] + dx[2][t], dz[1][t] + dy[2][t])
            for t in range(tiles)
        ]

    def stress(field, S, E):
        def body(x):
            strains = strain2(field, x)
            k = lax.shift_right_logical(x, 2)
            for t, e in enumerate(strains):
                rows_t = pl.ds(B * t, B)
                hl, mu = PF[0, k, rows_t], PF[1, k, rows_t]
                common = hl * (e[0] + e[1] + e[2])
                hm = 0.5 * mu
                for c in range(3):
                    S[c, x, rows_t] = common + mu * e[c]
                    S[3 + c, x, rows_t] = hm * e[3 + c]
            for c in range(6):
                E[c, x] = strains[0][c]
        return body

    def force2(S, x, tiles=2):
        y = [along_y(plane(S, c, x), tiles) for c in (3, 1, 5)]
        z = [along_z(plane(S, c, x), tiles) for c in (4, 5, 2)]
        d = [along_x(S, c, x, tiles=tiles) for c in (0, 3, 4)]
        return [[d[c][t] + y[c][t] + z[c][t] for c in range(3)] for t in range(tiles)]

    def advance(x):
        for t, f in enumerate(force2(S0, x)):
            rows_t = pl.ds(B * t, B)
            push = PF[2, lax.shift_right_logical(x, 2), rows_t]
            for c in range(3):
                A1[c, x, rows_t] = A[c, x, rows_t] + V[c, x, rows_t] + push * (f[c] + Q[c, x, rows_t])

    def forward_strain(x):
        for n in range(steps):
            (f,) = strain2(F.at[n + 1], x, 1)
            for c in range(6):
                FS[n, c, x] = f[c]

    def acceleration(x):
        for n in range(steps):
            for c in range(3):
                AC[n, c, x] = F[n + 2, c, x, 0:B] - 2.0 * F[n + 1, c, x, 0:B] + F[n, c, x, 0:B]

    scale = 1.0 / math.sqrt(ratio**3 * steps * n_ev)

    def kernel_sums(field, E, n):
        def body(x):
            e = [E[c, x] for c in range(6)]
            f = [FS[n, c, x] for c in range(6)]
            both = (e[0] + e[1] + e[2]) * (f[0] + f[1] + f[2])
            pure = 2.0 * (e[0] * f[0] + e[1] * f[1] + e[2] * f[2]) + (e[3] * f[3] + e[4] * f[4] + e[5] * f[5])
            move = field[0, x, 0:B] * AC[n, 0, x] + field[1, x, 0:B] * AC[n, 1, x] + field[2, x, 0:B] * AC[n, 2, x]
            for m, (v, w) in enumerate(((both, 0.25), (pure, 0.25), (move, 1.0))):
                v = v * (w * scale)
                KX[m, x] = v if n == 0 else KX[m, x] + v
        return body

    local[1].wait()
    bytes_of(S0.at[:, pl.ds(0, 3 * EXT // 4)], lsem.at[0]).wait()
    inner(0, B, acceleration)
    arrived(0, False)
    arrived(1, False)
    constants(0)
    inner(1, B - 1, stress(A, S0, E0))
    arrived(2, False)
    inner(2, B - 2, advance)
    inner(3, B - 3, stress(A1, S1, E1))
    arrived(3, False)
    inner(1, B - 1, forward_strain)
    inner(1, B - 1, kernel_sums(A, E0, 0))
    inner(3, B - 3, kernel_sums(A1, E1, 1))

    send_after_answer(3)

    arrived(0, True)
    constants(1)
    arrived(1, True)
    outer(1, B - 1, 3, stress(A, S0, E0))
    arrived(2, True)
    outer(2, B - 2, 2, advance)
    outer(3, B - 3, 1, stress(A1, S1, E1))
    arrived(3, True)
    outer(1, B - 1, 0, forward_strain)
    outer(1, B - 1, 0, kernel_sums(A, E0, 0))
    outer(3, B - 3, 0, kernel_sums(A1, E1, 1))

    sums = []
    for m in range(3):
        for k in range(B // ratio):
            v = sum(KX[m, ratio * k + j] for j in range(1, ratio)) + KX[m, ratio * k]
            v = v + pltpu.roll(v, B - 1, 0)
            sums.append(v + pltpu.roll(v, B - 2, 0))
    spot = lax.bitwise_and(sub, 3)
    halves = []
    for at in (0, 4):
        v = sums[at]
        for j in range(1, min(4, len(sums) - at)):
            v = jnp.where(spot == j, pltpu.roll(sums[at + j], j, 0), v)
        halves.append(v)
    wide = jnp.concatenate(halves, axis=1)
    wi = lax.broadcasted_iota(jnp.int32, (2 * depth, depth), 0)
    wj = lax.broadcasted_iota(jnp.int32, (2 * depth, depth), 1)
    T[...] = times_ones(wide, jnp.where(wi // ratio == wj, 1.0, 0.0))
    parts = [pltpu.make_async_remote_copy(
        src_ref=T, dst_ref=G.at[o - 1], send_sem=gsem.at[0], recv_sem=gsem.at[1],
        device_id={"event": lax.rem(ev + o, n_ev)}, device_id_type=MESH) for o in range(1, n_ev)]
    answered(2)
    for c in parts:
        c.start()

    def finish(x):
        (f,) = force2(S1, x, 1)
        push = PF[2, lax.shift_right_logical(x, 2), 0:B]
        for c in range(3):
            aend[0, c, x] = 2.0 * A1[c, x, 0:B] - A[c, x, 0:B] + push * (f[c] + Q[3 + c, x, 0:B])
    inner(0, B, finish)
    sent()
    bytes_of(G, gsem.at[0]).wait()
    bytes_of(G, gsem.at[1]).wait()
    total = T[...]
    for o in range(n_ev - 1):
        total = total + G[o]
    width = nzc // n_ev
    mine = pltpu.roll(total, lax.rem(depth - width * ev, depth), 1)
    other = pltpu.roll(mine, depth - nzc, 1)
    for m in range(3):
        for k in range(2):
            i = 2 * m + k
            src = mine if i < 4 else other
            for y in range(2):
                grad[m, k, y:y + 1] = src[4 * y + i % 4:4 * y + i % 4 + 1, 0:width]


def put_out(aend, grad, aend_out, grad_out, sems):
    copies = [pltpu.make_async_copy(aend, aend_out, sems.at[0]), pltpu.make_async_copy(grad, grad_out, sems.at[1])]
    for c in copies:
        c.start()
    for c in copies:
        c.wait()


def solution(mesh):
    n_gx, n_gy, n_ev = mesh.shape["gx"], mesh.shape["gy"], mesh.shape["event"]

    def on_device(adjoint, velocity, forward, receivers, residual, params):
        depth = adjoint.shape[-1]
        ratio = adjoint.shape[2] // params.shape[1]
        levels = forward.shape[1]
        steps = levels - 2
        nzc = params.shape[3]
        n_rec = receivers.shape[1]
        sizes = (n_gx, n_gy, n_ev, depth, ratio, steps)
        vm = pltpu.VMEM
        held = pl.pallas_call(
            functools.partial(kernel, sizes),
            out_shape=(
                pltpu.VMEM(adjoint.shape, F32),
                pltpu.VMEM((3, params.shape[1], params.shape[2], nzc // n_ev), F32),
            ),
            in_specs=[pl.BlockSpec(memory_space=pl.ANY)] * 6,
            out_specs=(pl.BlockSpec(memory_space=pltpu.VMEM), pl.BlockSpec(memory_space=pltpu.VMEM)),
            scratch_shapes=[
                vm((3, EXT, EXT, depth), F32),
                vm((3, EXT, EXT, depth), F32),
                vm((3, EXT, EXT, depth), F32),
                vm((levels, 3, EXT, EXT, depth), F32),
                vm((3, 4, 4, nzc), F32),
                vm((48, nzc), F32),
                vm((48, depth), F32),
                vm((3, 4, EXT, depth), F32),
                vm((1, n_rec), jnp.int32),
                vm((3, steps, n_rec), F32),
                vm((EXT * EXT, n_rec), BF16),
                vm((3 * steps, EXT, EXT, depth), F32),
                vm((6, EXT, EXT, depth), F32),
                vm((6, EXT, EXT, depth), F32),
                vm((6, EXT, B, depth), F32),
                vm((6, EXT, B, depth), F32),
                vm((steps, 6, B, B, depth), F32),
                vm((steps, 3, B, B, depth), F32),
                vm((3, B, B, depth), F32),
                vm((8, depth), F32),
                vm((n_ev - 1, 8, depth), F32),
                pltpu.SemaphoreType.DMA((4,)),
                pltpu.SemaphoreType.DMA((2, len(ORDER))),
                pltpu.SemaphoreType.DMA((2, len(ORDER))),
                pltpu.SemaphoreType.DMA((2, len(FACES))),
                pltpu.SemaphoreType.DMA((2,)),
                pltpu.SemaphoreType.REGULAR((4,)),
            ],
            compiler_params=pltpu.CompilerParams(collective_id=0, has_side_effects=True),
        )(adjoint, velocity, forward, receivers, jnp.swapaxes(residual, 1, 2), params)
        return pl.pallas_call(
            put_out,
            out_shape=tuple(jax.ShapeDtypeStruct(h.shape, F32) for h in held),
            in_specs=[pl.BlockSpec(memory_space=pltpu.VMEM)] * 2,
            out_specs=(pl.BlockSpec(memory_space=pl.ANY),) * 2,
            scratch_shapes=[pltpu.SemaphoreType.DMA((2,))],
        )(*[pltpu.with_memory_space_constraint(h, pltpu.VMEM) for h in held])

    return jax.shard_map(
        on_device,
        mesh=mesh,
        in_specs=(
            P("event", None, "gx", "gy", None),
            P("event", None, "gx", "gy", None),
            P("event", None, None, "gx", "gy", None),
            P("event", None),
            P("event", None, None, None),
            P(None, "gx", "gy", None),
        ),
        out_specs=(P("event", None, "gx", "gy", None), P(None, "gx", "gy", "event")),
        check_vma=False,
    )
```
